1024 devices in a mesh: section: 2 (over y_lo), scene: 32 (over z, core), mp: 16 (over x, y_hi).
Axes of the slice: x: 4, y: 8 (y_hi: 4, y_lo: 2; y = y_hi * 2 + y_lo), z: 16, core: 2. Of those that a mesh axis runs over, the one named last changes fastest.
Arguments:
- dec_grad: bfloat16 [32, 32, 256, 4096], P('scene', ('section', 'mp')), may hold values from -1.0546875 to 1.0546875
- agent_queries: bfloat16 [32, 256, 4096], P('scene', None, ('section', 'mp')), as said below
- map_keys: bfloat16 [32, 1024, 4096], P('scene', None, ('section', 'mp')), as said below
- map_values: bfloat16 [32, 1024, 4096], P('scene', None, ('section', 'mp')), may hold values from -6 to 6
- w_out: bfloat16 [4096, 4096], P(('section', 'mp'), 'scene'), may hold values from -0.09375 to 0.09375
- block_mask: int32 [32, 2, 8], P('scene'), may hold values from 0 to 1, as said below
- agent_count: int32 [32], P('scene'), may hold values from 64 to 256
Outputs:
- d_queries: bfloat16 [32, 256, 4096], P('scene', None, ('section', 'mp'))
- d_keys: bfloat16 [32, 1024, 4096], P('scene', None, ('section', 'mp'))
- d_values: bfloat16 [32, 1024, 4096], P('scene', None, ('section', 'mp'))
- d_wout: float32 [4096, 4096], P(('section', 'mp'), 'scene')
The draws below stay inside these ranges and needn't reach their ends.
Inputs may be any that keep to these rules, and one draw needn't show every extreme that they name: `block_mask`: every agent block of a scene sees map block 0. In each scene at most 4 map blocks are seen by some agent block, and some scene reaches 4. `agent_queries`: entries are finite and of moderate size. `map_keys`: entries are finite and of moderate size.
All inputs are finite; a program needn't handle non-finite values.
Results may differ from the reference program's by a relative error of at most 0.04.
Values may be sent and summed in bfloat16 or wider, within the bound.
No kernel may reach another device: no remote copies, remote signals or barrier semaphores. Data moves between devices by JAX's collectives and lax.ppermute only.
A program may use at most 32 MiB of HBM per device.

```python
import math
import jax
import jax.numpy as jnp
from jax import lax

D = 4096
HEAD_DIM = 128
HEADS = 32
BLOCK = 128
AGENT_TOK = 256
MAP_TOK = 1024
SAMP_DEV = 1
SAMPLES = 32
SCENES = 32
QBLOCKS = 2
MBLOCKS = 8
MAXLIVE = 4
N_SECTION = 2
N_MP = 16


def draw_agent_queries(key, part):
    base = jax.random.truncated_normal(jax.random.fold_in(key, 1), -6.0, 6.0, (SCENES, AGENT_TOK, D), jnp.float32)
    return base.astype(jnp.bfloat16)


def draw_map_keys(key, part):
    base = jax.random.truncated_normal(jax.random.fold_in(key, 2), -6.0, 6.0, (SCENES, MAP_TOK, D), jnp.float32)
    return base.astype(jnp.bfloat16)


def draw_block_mask(key, part):
    live_count = jax.random.randint(jax.random.fold_in(key, 11), (SCENES,), max(MAXLIVE // 2, 1), MAXLIVE + 1)
    fullest = jax.random.randint(jax.random.fold_in(key, 12), (), 0, SCENES)
    live_count = jnp.where(jnp.arange(SCENES) == fullest, MAXLIVE, live_count)
    scene_keys = jax.random.split(jax.random.fold_in(key, 13), SCENES)
    shuffled = jax.vmap(lambda one_key: jax.random.permutation(one_key, MBLOCKS - 1))(scene_keys)
    ranking = jnp.argsort(shuffled, axis=1)
    chosen = ranking < live_count[:, None] - 1
    union = jnp.concatenate([jnp.ones((SCENES, 1), dtype=bool), chosen], axis=1)
    coins = jax.random.randint(jax.random.fold_in(key, 14), (SCENES, QBLOCKS, MBLOCKS), 0, 2) == 1
    block_ids = jnp.arange(MBLOCKS)
    owner = block_ids[None, :] % QBLOCKS == jnp.arange(QBLOCKS)[:, None]
    forced = owner | (block_ids == 0)[None, :]
    visible = union[:, None, :] & (coins | forced[None])
    return visible.astype(jnp.int32)


def place_ends(drawn, key, low, top_value):
    extent = drawn.shape
    spot = [jax.random.randint(jax.random.fold_in(key, axis), (), 0, extent[axis]) for axis in range(len(extent))]
    drawn = drawn.at[tuple(spot)].set(low)
    longest = extent.index(max(extent))
    spot[longest] = (spot[longest] + 1) % extent[longest]
    return drawn.at[tuple(spot)].set(top_value)


def level_of(stream_key, dims, cuts, smallest, high):
    level = 1.0
    for position, blocks in cuts:
        draws = jax.random.uniform(jax.random.fold_in(jax.random.fold_in(stream_key, 6), position), (blocks,), jnp.float32, smallest / len(cuts), high / len(cuts))
        level = level * jnp.repeat(jnp.exp(draws), dims[position] // blocks).reshape((-1,) + (1,) * (len(dims) - 1 - position))
    return level


def scatter_about(own_key, dims, scale, reach, pieces=(), kind=jnp.bfloat16):
    drawn = scale * jax.random.normal(own_key, dims, jnp.float32)
    if pieces:
        drawn = drawn * level_of(own_key, dims, pieces, -0.22, 0.18)
    return jnp.clip(drawn, -reach, reach).astype(kind)


def setup_inputs(seed: int = 0) -> dict:
    keys = jax.random.split(jax.random.key(seed), 8)
    return {
        "dec_grad": scatter_about(keys[0], (SCENES, SAMPLES, AGENT_TOK, D), (SAMPLES ** -0.5), 1.0546875, ((0, 32), (1, 32))),
        "agent_queries": draw_agent_queries(jax.random.fold_in(keys[7], 71), 0),
        "map_keys": draw_map_keys(jax.random.fold_in(keys[7], 71), 0),
        "map_values": scatter_about(keys[3], (SCENES, MAP_TOK, D), 1.0, 6.0, ((0, 32), (2, 32))),
        "w_out": scatter_about(keys[4], (D, D), D ** -0.5, 0.09375, ((0, 32), (1, 32))),
        "block_mask": draw_block_mask(jax.random.fold_in(keys[7], 71), 0),
        "agent_count": place_ends(jax.random.randint(keys[6], (SCENES,), AGENT_TOK // 4, AGENT_TOK + 1), jax.random.fold_in(keys[6], 1), AGENT_TOK // 4, AGENT_TOK).astype(jnp.int32),
    }


def reference(dec_grad, agent_queries, map_keys, map_values, w_out, block_mask, agent_count):
    device_groups = N_SECTION * N_MP
    scaling = 1.0 / math.sqrt(HEAD_DIM)

    def one_scene(weight_grad, inputs):
        sample_grads, queries, key_rows, value_rows, mask_rows, agent_total = inputs
        grouped = sample_grads.reshape(device_groups, SAMP_DEV, AGENT_TOK, D).astype(jnp.float32)
        partial_value = lax.optimization_barrier(jnp.sum(grouped, axis=1)).astype(jnp.bfloat16)
        summed = lax.optimization_barrier(jnp.sum(partial_value.astype(jnp.float32), axis=0))
        row_keep = jnp.arange(AGENT_TOK) < agent_total
        upstream = jnp.where(row_keep[:, None], summed, 0.0).astype(jnp.bfloat16)
        d_attn = jnp.dot(upstream, w_out.T, preferred_element_type=jnp.float32).astype(jnp.bfloat16)
        visible = jnp.repeat(jnp.repeat(mask_rows == 1, BLOCK, axis=0), BLOCK, axis=1)
        query_heads = queries.reshape(AGENT_TOK, HEADS, HEAD_DIM).astype(jnp.float32)
        key_heads = key_rows.reshape(MAP_TOK, HEADS, HEAD_DIM).astype(jnp.float32)
        value_heads = value_rows.reshape(MAP_TOK, HEADS, HEAD_DIM).astype(jnp.float32)
        grad_heads = d_attn.reshape(AGENT_TOK, HEADS, HEAD_DIM).astype(jnp.float32)
        scores = jnp.einsum('qhd,khd->hqk', query_heads, key_heads) * scaling
        scores = jnp.where(visible[None], scores, -1e+30)
        largest = lax.optimization_barrier(jnp.max(scores, axis=-1, keepdims=True))
        exponent = jnp.exp(scores - largest)
        probs = exponent / lax.optimization_barrier(jnp.sum(exponent, axis=-1, keepdims=True))
        weights = lax.optimization_barrier(probs.astype(jnp.bfloat16)).astype(jnp.float32)
        attended = jnp.einsum('hqk,khd->qhd', weights, value_heads)
        attended_rounded = attended.astype(jnp.bfloat16)
        weight_grad = weight_grad + jnp.dot(attended_rounded.reshape(AGENT_TOK, D).T, upstream, preferred_element_type=jnp.float32)
        delta = lax.optimization_barrier(jnp.sum(grad_heads * attended, axis=-1))
        d_values = jnp.einsum('hqk,qhd->khd', weights, grad_heads).astype(jnp.bfloat16)
        d_probs = jnp.einsum('qhd,khd->hqk', grad_heads, value_heads)
        d_scores = probs * (d_probs - delta.T[:, :, None])
        score_grads = lax.optimization_barrier(d_scores.astype(jnp.bfloat16)).astype(jnp.float32)
        d_queries = (scaling * jnp.einsum('hqk,khd->qhd', score_grads, key_heads)).astype(jnp.bfloat16)
        d_keys = (scaling * jnp.einsum('hqk,qhd->khd', score_grads, query_heads)).astype(jnp.bfloat16)
        return (weight_grad, (d_queries.reshape(AGENT_TOK, D), d_keys.reshape(MAP_TOK, D), d_values.reshape(MAP_TOK, D)))
    initial = jnp.zeros((D, D), jnp.float32)
    d_wout, outputs = lax.scan(one_scene, initial, (dec_grad, agent_queries, map_keys, map_values, block_mask, agent_count))
    d_queries, d_keys, d_values = outputs
    return (d_queries, d_keys, d_values, d_wout)
```

```python
import math

import jax
import jax.numpy as jnp
from jax import lax
from jax.experimental import pallas as pl
from jax.experimental.pallas import tpu as pltpu
from jax.sharding import PartitionSpec as P

HEAD_DIM = 128
XY = ("section", "mp")
X, YH, YL = 4, 4, 2
ZH, ZL, CORES = 4, 4, 2


def xy_index(x, y):
    return (y % YL) * (X * YH) + x * YH + y // YL


def scene_index(zh, zl, core):
    return (zh * ZL + zl) * CORES + core


def shift_x(k):
    return [(x * YH + y, ((x + k) % X) * YH + y) for x in range(X) for y in range(YH)]


def shift_zl(k):
    return [
        (scene_index(a, b, c), scene_index(a, (b + k) % ZL, c))
        for a in range(ZH)
        for b in range(ZL)
        for c in range(CORES)
    ]


def shift_zh(k):
    return [
        (scene_index(a, b, c), scene_index((a + k) % ZH, b, c))
        for a in range(ZH)
        for b in range(ZL)
        for c in range(CORES)
    ]


def other_core():
    return [(s, s ^ 1) for s in range(ZH * ZL * CORES)]


def y_groups():
    return [[xy_index(x, y) for y in range(YH * YL)] for x in range(X)]


def z_groups():
    return [[z * CORES + c for z in range(ZH * ZL)] for c in range(CORES)]


def attend_forward(queries, keys, values, visible, scaling):
    scores = jnp.einsum("qd,kd->qk", queries, keys, preferred_element_type=jnp.float32) * scaling
    scores = jnp.where(visible, scores, -1e30)
    largest = jnp.max(scores, axis=-1, keepdims=True)
    exponent = jnp.exp(scores - largest)
    probs = exponent / jnp.sum(exponent, axis=-1, keepdims=True)
    weights = probs.astype(jnp.bfloat16)
    attended = jnp.einsum("qk,kd->qd", weights, values, preferred_element_type=jnp.float32)
    return probs, weights, attended


def attend_backward(queries, keys, values, grads, probs, weights, attended, scaling):
    delta = jnp.sum(grads.astype(jnp.float32) * attended, axis=-1)
    d_values = jnp.einsum("qk,qd->kd", weights, grads, preferred_element_type=jnp.float32)
    d_probs = jnp.einsum("qd,kd->qk", grads, values, preferred_element_type=jnp.float32)
    score_grads = (probs * (d_probs - delta[:, None])).astype(jnp.bfloat16)
    d_queries = scaling * jnp.einsum(
        "qk,kd->qd", score_grads, keys, preferred_element_type=jnp.float32
    )
    d_keys = scaling * jnp.einsum(
        "qk,qd->kd", score_grads, queries, preferred_element_type=jnp.float32
    )
    return [g.astype(jnp.bfloat16) for g in (d_queries, d_keys, d_values)]


def weight_terms_kernel(core_ref, attended_ref, *refs):
    blocks, (send_ref, keep_ref) = refs[:X], refs[X:]
    first = core_ref[0] == 0
    for k in range(X):
        term = lax.dot_general(
            attended_ref[...],
            blocks[k][...],
            (((0,), (0,)), ((), ())),
            preferred_element_type=jnp.float32,
        )
        for b in range(ZL):
            left = b * CORES * HEAD_DIM
            low = term[:, left : left + HEAD_DIM]
            high = term[:, left + HEAD_DIM : left + 2 * HEAD_DIM]
            send_ref[b, k] = jnp.where(first, high, low).astype(jnp.bfloat16)
            keep_ref[b, k] = jnp.where(first, low, high)


def weight_terms(core, attended, blocks):
    rows, width = blocks[0].shape
    shape = (ZL, X, HEAD_DIM, HEAD_DIM)
    vmem = pl.BlockSpec(memory_space=pltpu.VMEM)
    return pl.pallas_call(
        weight_terms_kernel,
        out_shape=(
            jax.ShapeDtypeStruct(shape, jnp.bfloat16),
            jax.ShapeDtypeStruct(shape, jnp.float32),
        ),
        in_specs=[pl.BlockSpec(memory_space=pltpu.SMEM)] + [vmem] * (1 + X),
        out_specs=(vmem, vmem),
        compiler_params=pltpu.CompilerParams(vmem_limit_bytes=24 << 20),
        cost_estimate=pl.CostEstimate(
            flops=2 * rows * width * X * HEAD_DIM,
            bytes_accessed=2 * rows * width * X + 6 * width * X * HEAD_DIM // 2,
            transcendentals=0,
        ),
        name="weight_terms",
    )(core.reshape(1), attended, *blocks)


def shift_right(number, size):
    return lax.shift_right_logical(number, size.bit_length() - 1)


def sum_f32(parts):
    total = parts[0].astype(jnp.float32)
    for part in parts[1:]:
        total = total + part.astype(jnp.float32)
    return total


def shards(dec_grad, agent_queries, map_keys, map_values, w_out, block_mask, agent_count):
    scaling = 1.0 / math.sqrt(HEAD_DIM)
    section, mp, scene = (lax.axis_index(name) for name in ("section", "mp", "scene"))
    x, y = shift_right(mp, YH), (mp & (YH - 1)) * YL + section
    zh, zl = shift_right(scene, ZL * CORES), shift_right(scene, CORES) & (ZL - 1)
    core = scene & (CORES - 1)
    sample = dec_grad[0, 0]
    tokens, model = sample.shape
    width = model // X

    with jax.named_scope("gather_projection"):
        w_other = lax.ppermute(w_out, "scene", other_core())
        w_chip = jnp.concatenate(
            [jnp.where(core == 0, w_out, w_other), jnp.where(core == 0, w_other, w_out)], axis=1
        )
        w_full = lax.all_gather(w_chip, "scene", axis=1, tiled=True, axis_index_groups=z_groups())

    with jax.named_scope("sum_over_x"):
        pieces = [
            lax.dynamic_slice(sample, (0, ((x + k) & (X - 1)) * width), (tokens, width))
            for k in range(X)
        ]
        arrived = [lax.ppermute(pieces[k], "mp", shift_x(k)) for k in range(1, X)]
        partial = sum_f32([pieces[0]] + arrived).astype(jnp.bfloat16)

    queries, keys, values = agent_queries[0], map_keys[0], map_values[0]
    mask_rows = block_mask[0]
    agent_block, map_block = tokens // mask_rows.shape[0], keys.shape[0] // mask_rows.shape[1]
    visible = jnp.repeat(jnp.repeat(mask_rows == 1, agent_block, axis=0), map_block, axis=1)
    probs, weights, attended = attend_forward(queries, keys, values, visible, scaling)
    attended_rounded = attended.astype(jnp.bfloat16)

    with jax.named_scope("sum_over_y"):
        rows = tokens // (YH * YL)
        lines = lax.all_to_all(
            partial.reshape(YH * YL, rows, width), XY, 0, 0, axis_index_groups=y_groups()
        )
        summed = jnp.sum(lines.astype(jnp.float32), axis=0)
        row_keep = y * rows + jnp.arange(rows) < agent_count[0]
        own = jnp.where(row_keep[:, None], summed, 0.0).astype(jnp.bfloat16)

    with jax.named_scope("gather_over_y"):
        spread = jnp.broadcast_to(own[None], (YH * YL, rows, width))
        block = lax.all_to_all(spread, XY, 0, 0, axis_index_groups=y_groups())
        block = block.reshape(tokens, width)

    with jax.named_scope("gather_over_x"):
        upstream = [block] + [lax.ppermute(block, "mp", shift_x(-k)) for k in range(1, X)]

    with jax.named_scope("weight_terms"):
        send, keep = weight_terms(core, attended_rounded, upstream)

    with jax.named_scope("sum_over_core"):
        pair = sum_f32([keep, lax.ppermute(send, "scene", other_core())]).astype(jnp.bfloat16)

    with jax.named_scope("sum_over_z_lo"):
        parts = [
            lax.dynamic_index_in_dim(pair, (zl + k) & (ZL - 1), 0, keepdims=False) for k in range(ZL)
        ]
        near = sum_f32(
            parts[:1] + [lax.ppermute(parts[k], "scene", shift_zl(k)) for k in range(1, ZL)]
        ).astype(jnp.bfloat16)

    with jax.named_scope("sum_over_z_hi"):
        parts = [
            lax.dynamic_index_in_dim(near, (zh + k - x) & (X - 1), 0, keepdims=False)
            for k in range(ZH)
        ]
        d_wout = sum_f32(
            parts[:1] + [lax.ppermute(parts[k], "scene", shift_zh(k)) for k in range(1, ZH)]
        )

    with jax.named_scope("head_gradients"):
        upstream, w_full, _ = lax.optimization_barrier((upstream, w_full, pair))
        d_attn = sum(
            jnp.einsum(
                "td,hd->th",
                upstream[k],
                lax.dynamic_slice(w_full, (0, ((x + k) & (X - 1)) * width), (HEAD_DIM, width)),
                preferred_element_type=jnp.float32,
            )
            for k in range(X)
        ).astype(jnp.bfloat16)
        d_queries, d_keys, d_values = attend_backward(
            queries, keys, values, d_attn, probs, weights, attended, scaling
        )
    return d_queries[None], d_keys[None], d_values[None], d_wout


def solution(mesh):
    heads = P("scene", None, XY)
    return jax.shard_map(
        shards,
        mesh=mesh,
        in_specs=(
            P("scene", XY, None, None),
            heads,
            heads,
            heads,
            P(XY, "scene"),
            P("scene", None, None),
            P("scene"),
        ),
        out_specs=(heads, heads, heads, P(XY, "scene")),
        check_vma=False,
    )
```

```python
import math

import jax
import jax.numpy as jnp
from jax import lax
from jax.experimental import pallas as pl
from jax.experimental.pallas import tpu as pltpu
from jax.sharding import PartitionSpec as P

HEAD_DIM = 128
XY = ("section", "mp")
X, YH, YL = 4, 4, 2
ZH, ZL, CORES = 4, 4, 2


def xy_index(x, y):
    return (y % YL) * (X * YH) + x * YH + y // YL


def scene_index(zh, zl, core):
    return (zh * ZL + zl) * CORES + core


def shift_x(k):
    return [(x * YH + y, ((x + k) % X) * YH + y) for x in range(X) for y in range(YH)]


def shift_zl(k):
    return [
        (scene_index(a, b, c), scene_index(a, (b + k) % ZL, c))
        for a in range(ZH)
        for b in range(ZL)
        for c in range(CORES)
    ]


def shift_zh(k):
    return [
        (scene_index(a, b, c), scene_index((a + k) % ZH, b, c))
        for a in range(ZH)
        for b in range(ZL)
        for c in range(CORES)
    ]


def swap_x_zh():
    pairs = []
    for a in range(ZH):
        for rest in range(ZL * CORES):
            for x in range(X):
                for yh in range(YH):
                    here = ((a * ZL * CORES + rest) * X + x) * YH + yh
                    there = ((x * ZL * CORES + rest) * X + a) * YH + yh
                    pairs.append((here, there))
    return pairs


def other_core():
    return [(s, s ^ 1) for s in range(ZH * ZL * CORES)]


def y_groups():
    return [[xy_index(x, y) for y in range(YH * YL)] for x in range(X)]


def attend_forward(queries, keys, values, visible, scaling):
    scores = jnp.einsum("qd,kd->qk", queries, keys, preferred_element_type=jnp.float32) * scaling
    scores = jnp.where(visible, scores, -1e30)
    largest = jnp.max(scores, axis=-1, keepdims=True)
    exponent = jnp.exp(scores - largest)
    probs = exponent / jnp.sum(exponent, axis=-1, keepdims=True)
    weights = probs.astype(jnp.bfloat16)
    attended = jnp.einsum("qk,kd->qd", weights, values, preferred_element_type=jnp.float32)
    return probs, weights, attended


def attend_backward(queries, keys, values, grads, probs, weights, attended, scaling):
    delta = jnp.sum(grads.astype(jnp.float32) * attended, axis=-1)
    d_values = jnp.einsum("qk,qd->kd", weights, grads, preferred_element_type=jnp.float32)
    d_probs = jnp.einsum("qd,kd->qk", grads, values, preferred_element_type=jnp.float32)
    score_grads = (probs * (d_probs - delta[:, None])).astype(jnp.bfloat16)
    d_queries = scaling * jnp.einsum(
        "qk,kd->qd", score_grads, keys, preferred_element_type=jnp.float32
    )
    d_keys = scaling * jnp.einsum(
        "qk,qd->kd", score_grads, queries, preferred_element_type=jnp.float32
    )
    return [g.astype(jnp.bfloat16) for g in (d_queries, d_keys, d_values)]


def weight_terms_kernel(core_ref, block_ref, *refs):
    attended, (send_ref, keep_ref) = refs[:X], refs[X:]
    first = core_ref[0] == 0
    for k in range(X):
        term = lax.dot_general(
            attended[k][...],
            block_ref[...],
            (((0,), (0,)), ((), ())),
            preferred_element_type=jnp.float32,
        )
        for b in range(ZL):
            left = b * CORES * HEAD_DIM
            low = term[:, left : left + HEAD_DIM]
            high = term[:, left + HEAD_DIM : left + 2 * HEAD_DIM]
            send_ref[b, k] = jnp.where(first, high, low).astype(jnp.bfloat16)
            keep_ref[b, k] = jnp.where(first, low, high)


def weight_terms(core, block, attended):
    rows, width = block.shape
    shape = (ZL, X, HEAD_DIM, HEAD_DIM)
    vmem = pl.BlockSpec(memory_space=pltpu.VMEM)
    return pl.pallas_call(
        weight_terms_kernel,
        out_shape=(
            jax.ShapeDtypeStruct(shape, jnp.bfloat16),
            jax.ShapeDtypeStruct(shape, jnp.float32),
        ),
        in_specs=[pl.BlockSpec(memory_space=pltpu.SMEM)] + [vmem] * (1 + X),
        out_specs=(vmem, vmem),
        compiler_params=pltpu.CompilerParams(vmem_limit_bytes=24 << 20),
        cost_estimate=pl.CostEstimate(
            flops=2 * rows * width * X * HEAD_DIM,
            bytes_accessed=2 * rows * (width + X * HEAD_DIM) + 3 * width * X * HEAD_DIM,
            transcendentals=0,
        ),
        name="weight_terms",
    )(core.reshape(1), block, *attended)


def head_grad_kernel(place_ref, *refs):
    blocks, weights, out_ref = refs[:X], refs[X : X + ZL], refs[X + ZL]
    x, zh, zl = place_ref[0], place_ref[1], place_ref[2]
    wide = CORES * HEAD_DIM
    total = jnp.zeros(out_ref.shape, jnp.float32)
    for k in range(X):
        far = (x + k - zh) & (ZH - 1)
        for i in range(ZL):
            left = pl.multiple_of(((zl + i) & (ZL - 1)) * wide, wide)
            total += lax.dot_general(
                blocks[k][:, pl.ds(left, wide)],
                weights[i][far],
                (((1,), (1,)), ((), ())),
                preferred_element_type=jnp.float32,
            )
    out_ref[...] = total.astype(out_ref.dtype)


def head_grad(place, blocks, weights):
    rows, width = blocks[0].shape
    vmem = pl.BlockSpec(memory_space=pltpu.VMEM)
    return pl.pallas_call(
        head_grad_kernel,
        out_shape=jax.ShapeDtypeStruct((rows, HEAD_DIM), jnp.bfloat16),
        in_specs=[pl.BlockSpec(memory_space=pltpu.SMEM)] + [vmem] * (X + ZL),
        out_specs=vmem,
        compiler_params=pltpu.CompilerParams(vmem_limit_bytes=24 << 20),
        cost_estimate=pl.CostEstimate(
            flops=2 * rows * width * X * HEAD_DIM,
            bytes_accessed=2 * (rows + HEAD_DIM) * width * X,
            transcendentals=0,
        ),
        name="head_grad",
    )(place, *blocks, *weights)


def shift_right(number, size):
    return lax.shift_right_logical(number, size.bit_length() - 1)


def sum_f32(parts):
    total = parts[0].astype(jnp.float32)
    for part in parts[1:]:
        total = total + part.astype(jnp.float32)
    return total


def shards(dec_grad, agent_queries, map_keys, map_values, w_out, block_mask, agent_count):
    scaling = 1.0 / math.sqrt(HEAD_DIM)
    section, mp, scene = (lax.axis_index(name) for name in ("section", "mp", "scene"))
    x, y = shift_right(mp, YH), (mp & (YH - 1)) * YL + section
    zh, zl = shift_right(scene, ZL * CORES), shift_right(scene, CORES) & (ZL - 1)
    core = scene & (CORES - 1)
    sample = dec_grad[0, 0]
    tokens, model = sample.shape
    width = model // X

    with jax.named_scope("sum_over_x"):
        pieces = [
            lax.dynamic_slice(sample, (0, ((x + k) & (X - 1)) * width), (tokens, width))
            for k in range(X)
        ]
        arrived = [lax.ppermute(pieces[k], "mp", shift_x(k)) for k in range(1, X)]
        partial = sum_f32([pieces[0]] + arrived).astype(jnp.bfloat16)

    with jax.named_scope("gather_projection"):
        w_other = lax.ppermute(w_out, "scene", other_core())
        w_chip = jnp.concatenate(
            [jnp.where(core == 0, w_out, w_other), jnp.where(core == 0, w_other, w_out)], axis=1
        )
        w_far = jnp.stack(
            [w_chip] + [lax.ppermute(w_chip, "scene", shift_zh(-k)) for k in range(1, ZH)]
        )

    queries, keys, values = agent_queries[0], map_keys[0], map_values[0]
    mask_rows = block_mask[0]
    agent_block, map_block = tokens // mask_rows.shape[0], keys.shape[0] // mask_rows.shape[1]
    visible = jnp.repeat(jnp.repeat(mask_rows == 1, agent_block, axis=0), map_block, axis=1)
    probs, weights, attended = attend_forward(queries, keys, values, visible, scaling)
    attended_rounded = attended.astype(jnp.bfloat16)

    partial, w_far, attended_rounded = lax.optimization_barrier((partial, w_far, attended_rounded))
    with jax.named_scope("sum_over_y"):
        rows = tokens // (YH * YL)
        lines = lax.all_to_all(
            partial.reshape(YH * YL, rows, width), XY, 0, 0, axis_index_groups=y_groups()
        )
        summed = jnp.sum(lines.astype(jnp.float32), axis=0)
        row_keep = y * rows + jnp.arange(rows) < agent_count[0]
        own = jnp.where(row_keep[:, None], summed, 0.0).astype(jnp.bfloat16)
    with jax.named_scope("gather_attended"):
        attended_near = [attended_rounded] + [
            lax.ppermute(attended_rounded, "mp", shift_x(-k)) for k in range(1, X)
        ]

    own, attended_near, w_far = lax.optimization_barrier((own, attended_near, w_far))
    with jax.named_scope("gather_over_y"):
        spread = jnp.broadcast_to(own[None], (YH * YL, rows, width))
        block = lax.all_to_all(spread, XY, 0, 0, axis_index_groups=y_groups())
        block = block.reshape(tokens, width)
    with jax.named_scope("gather_projection"):
        w_near = [w_far] + [lax.ppermute(w_far, "scene", shift_zl(-k)) for k in range(1, ZL)]

    block, w_near = lax.optimization_barrier((block, w_near))
    with jax.named_scope("weight_terms"):
        send, keep = weight_terms(core, block, attended_near)

    with jax.named_scope("sum_over_core"):
        pair = sum_f32([keep, lax.ppermute(send, "scene", other_core())]).astype(jnp.bfloat16)

    with jax.named_scope("gather_over_x"):
        upstream = [block] + [lax.ppermute(block, "mp", shift_x(-k)) for k in range(1, X)]

    with jax.named_scope("sum_over_z_lo"):
        parts = [
            lax.dynamic_index_in_dim(pair, (zl + k) & (ZL - 1), 0, keepdims=False)
            for k in range(ZL)
        ]
        near = sum_f32(
            parts[:1] + [lax.ppermute(parts[k], "scene", shift_zl(k)) for k in range(1, ZL)]
        ).astype(jnp.bfloat16)

    near, upstream, w_near = lax.optimization_barrier((near, upstream, w_near))
    with jax.named_scope("sum_over_z_hi"):
        parts = [
            lax.dynamic_index_in_dim(near, (zh + k - x) & (X - 1), 0, keepdims=False)
            for k in range(ZH)
        ]
        summed_block = sum_f32(
            parts[:1] + [lax.ppermute(parts[k], "scene", shift_zh(k)) for k in range(1, ZH)]
        )
        d_wout = lax.ppermute(summed_block, ("scene", "mp"), swap_x_zh())

    with jax.named_scope("head_gradients"):
        d_attn = head_grad(jnp.stack([x, zh, zl]), upstream, w_near)
        d_queries, d_keys, d_values = attend_backward(
            queries, keys, values, d_attn, probs, weights, attended, scaling
        )
    return d_queries[None], d_keys[None], d_values[None], d_wout


def solution(mesh):
    heads = P("scene", None, XY)
    return jax.shard_map(
        shards,
        mesh=mesh,
        in_specs=(
            P("scene", XY, None, None),
            heads,
            heads,
            heads,
            P(XY, "scene"),
            P("scene", None, None),
            P("scene"),
        ),
        out_specs=(heads, heads, heads, P(XY, "scene")),
        check_vma=False,
    )
```

```python
import math

import jax
import jax.numpy as jnp
from jax import lax
from jax.experimental import pallas as pl
from jax.experimental.pallas import tpu as pltpu
from jax.sharding import PartitionSpec as P

HEAD_DIM = 128
XY = ("section", "mp")
X, YH, YL = 4, 4, 2
ZH, ZL, CORES = 4, 4, 2


def xy_index(x, y):
    return (y % YL) * (X * YH) + x * YH + y // YL


def scene_index(zh, zl, core):
    return (zh * ZL + zl) * CORES + core


def shift_x(k):
    return [(x * YH + y, ((x + k) % X) * YH + y) for x in range(X) for y in range(YH)]


def shift_zl(k):
    return [
        (scene_index(a, b, c), scene_index(a, (b + k) % ZL, c))
        for a in range(ZH)
        for b in range(ZL)
        for c in range(CORES)
    ]


def shift_zh(k):
    return [
        (scene_index(a, b, c), scene_index((a + k) % ZH, b, c))
        for a in range(ZH)
        for b in range(ZL)
        for c in range(CORES)
    ]


def y_groups():
    return [[xy_index(x, y) for y in range(YH * YL)] for x in range(X)]


def z_hi_groups():
    return [
        [scene_index(a, b, c) for a in range(ZH)] for b in range(ZL) for c in range(CORES)
    ]


def other_core():
    return [(s, s ^ 1) for s in range(ZH * ZL * CORES)]


def swap_head_and_scene():
    def index(head, scene):
        x, yh, yl = head
        return (yl * ZH * ZL * CORES + scene_index(*scene)) * X * YH + x * YH + yh

    heads = [(x, yh, yl) for x in range(X) for yh in range(YH) for yl in range(YL)]
    return [(index(h, s), index(s, h)) for h in heads for s in heads]


def exchange(blocks, axis, groups):
    return lax.all_to_all(blocks, axis, 0, 0, axis_index_groups=groups)


def gather(block, axis, groups):
    return exchange(jnp.broadcast_to(block[None], (len(groups[0]), *block.shape)), axis, groups)


def ring_gather(block, axis, shift, size):
    return [block] + [lax.ppermute(block, axis, shift(-k)) for k in range(1, size)]


def ring_exchange(blocks, axis, shift):
    return blocks[:1] + [lax.ppermute(b, axis, shift(k)) for k, b in enumerate(blocks) if k]


def attend_forward(queries, keys, values, visible, scaling):
    scores = jnp.einsum("qd,kd->qk", queries, keys, preferred_element_type=jnp.float32) * scaling
    scores = jnp.where(visible, scores, -1e30)
    largest = jnp.max(scores, axis=-1, keepdims=True)
    exponent = jnp.exp(scores - largest)
    probs = exponent / jnp.sum(exponent, axis=-1, keepdims=True)
    weights = probs.astype(jnp.bfloat16)
    attended = jnp.einsum("qk,kd->qd", weights, values, preferred_element_type=jnp.float32)
    return probs, weights, attended


def attend_backward(queries, keys, values, grads, probs, weights, attended, scaling):
    delta = jnp.sum(grads.astype(jnp.float32) * attended, axis=-1)
    d_values = jnp.einsum("qk,qd->kd", weights, grads, preferred_element_type=jnp.float32)
    d_probs = jnp.einsum("qd,kd->qk", grads, values, preferred_element_type=jnp.float32)
    score_grads = (probs * (d_probs - delta[:, None])).astype(jnp.bfloat16)
    d_queries = scaling * jnp.einsum(
        "qk,kd->qd", score_grads, keys, preferred_element_type=jnp.float32
    )
    d_keys = scaling * jnp.einsum(
        "qk,qd->kd", score_grads, queries, preferred_element_type=jnp.float32
    )
    return [g.astype(jnp.bfloat16) for g in (d_queries, d_keys, d_values)]


VMEM = pl.BlockSpec(memory_space=pltpu.VMEM)
SMEM = pl.BlockSpec(memory_space=pltpu.SMEM)


def cost(flops, count):
    return pl.CostEstimate(flops=flops, bytes_accessed=count, transcendentals=0)


def split_sum_kernel(*refs):
    *part_refs, out_ref = refs
    for y in range(YH * YL):
        left = y * HEAD_DIM
        total = part_refs[0][:, left : left + HEAD_DIM].astype(jnp.float32)
        for part_ref in part_refs[1:]:
            total += part_ref[:, left : left + HEAD_DIM].astype(jnp.float32)
        out_ref[y] = total.astype(out_ref.dtype)


def split_sum(parts):
    tokens = parts[0].shape[0]
    return pl.pallas_call(
        split_sum_kernel,
        out_shape=jax.ShapeDtypeStruct((YH * YL, tokens, HEAD_DIM), jnp.bfloat16),
        in_specs=[VMEM] * len(parts),
        out_specs=VMEM,
        compiler_params=pltpu.CompilerParams(vmem_limit_bytes=16 << 20),
        cost_estimate=cost(parts[0].size * len(parts), 2 * parts[0].size * (len(parts) + 1)),
        name="split_sum",
    )(*parts)


def weight_terms_kernel(place_ref, own_ref, *refs):
    attended_refs, (send_ref, keep_ref) = refs[:X], refs[X:]
    first = place_ref[0] == 0
    for k in range(X):
        x = (place_ref[1] + k) & (X - 1)
        for yh in range(YH):
            low, high = [
                jnp.dot(
                    attended_refs[k][yh * YL + yl],
                    own_ref[...],
                    preferred_element_type=jnp.float32,
                )
                for yl in range(YL)
            ]
            send_ref[yh, x] = jnp.where(first, high, low).astype(jnp.bfloat16)
            keep_ref[yh, x] = jnp.where(first, low, high)


def weight_terms(place, attended, own):
    tokens, columns = own.shape
    shape = (YH, X, HEAD_DIM, columns)
    size = attended[0].size * X
    return pl.pallas_call(
        weight_terms_kernel,
        out_shape=(
            jax.ShapeDtypeStruct(shape, jnp.bfloat16),
            jax.ShapeDtypeStruct(shape, jnp.float32),
        ),
        in_specs=[SMEM] + [VMEM] * (1 + X),
        out_specs=(VMEM, VMEM),
        compiler_params=pltpu.CompilerParams(vmem_limit_bytes=24 << 20),
        cost_estimate=cost(2 * size * columns, 2 * size + 6 * YH * X * HEAD_DIM * columns),
        name="weight_terms",
    )(place, own, *attended)


def head_grad_kernel(place_ref, w_own_ref, w_other_ref, *refs):
    *upstream_refs, out_ref = refs
    core, x, zh, zl = [place_ref[i] for i in range(4)]
    total = jnp.zeros(out_ref.shape, jnp.float32)
    for k in range(X):
        far = (x + k - zh) & (ZH - 1)
        for b in range(ZL):
            near = (b - zl) & (ZL - 1)
            for w_ref, c in ((w_own_ref, core), (w_other_ref, 1 - core)):
                total += lax.dot_general(
                    upstream_refs[k][b * CORES + c],
                    w_ref[near, far],
                    (((1,), (1,)), ((), ())),
                    preferred_element_type=jnp.float32,
                )
    out_ref[...] = total.astype(out_ref.dtype)


def head_grad(place, upstream, w_own, w_other):
    tokens = upstream[0].shape[1]
    size = upstream[0].size * X
    return pl.pallas_call(
        head_grad_kernel,
        out_shape=jax.ShapeDtypeStruct((tokens, HEAD_DIM), jnp.bfloat16),
        in_specs=[SMEM] + [VMEM] * (2 + X),
        out_specs=VMEM,
        compiler_params=pltpu.CompilerParams(vmem_limit_bytes=24 << 20),
        cost_estimate=cost(2 * size * HEAD_DIM, 2 * (size + 2 * w_own.size)),
        name="head_grad",
    )(place, w_own, w_other, *upstream)


def shift_right(number, size):
    return lax.shift_right_logical(number, size.bit_length() - 1)


def sum_f32(parts):
    total = parts[0].astype(jnp.float32)
    for k in range(1, len(parts)):
        total = total + parts[k].astype(jnp.float32)
    return total


def shards(dec_grad, agent_queries, map_keys, map_values, w_out, block_mask, agent_count):
    scaling = 1.0 / math.sqrt(HEAD_DIM)
    mp, scene = lax.axis_index("mp"), lax.axis_index("scene")
    x, core = shift_right(mp, YH), scene & (CORES - 1)
    zh, zl = shift_right(scene, ZL * CORES), shift_right(scene, CORES) & (ZL - 1)
    place = jnp.stack([core, x, zh, zl])
    sample = dec_grad[0, 0]
    tokens, model = sample.shape
    width = model // X

    with jax.named_scope("sum_over_x"):
        pieces = [
            lax.dynamic_slice(sample, (0, ((x + k) & (X - 1)) * width), (tokens, width))
            for k in range(X)
        ]
        partial = split_sum(ring_exchange(pieces, "mp", shift_x))

    with jax.named_scope("gather_projection"):
        w_far = jnp.stack(ring_gather(w_out, "scene", shift_zh, ZH))

    queries, keys, values = agent_queries[0], map_keys[0], map_values[0]
    mask_rows = block_mask[0]
    agent_block, map_block = tokens // mask_rows.shape[0], keys.shape[0] // mask_rows.shape[1]
    visible = jnp.repeat(jnp.repeat(mask_rows == 1, agent_block, axis=0), map_block, axis=1)
    probs, weights, attended = attend_forward(queries, keys, values, visible, scaling)
    with jax.named_scope("gather_attended"):
        attended_near = gather(attended.astype(jnp.bfloat16).T, XY, y_groups())

    partial, attended_near = lax.optimization_barrier((partial, attended_near))
    with jax.named_scope("sum_over_y"):
        summed = sum_f32(exchange(partial, XY, y_groups()))
        row_keep = jnp.arange(tokens) < agent_count[0]
        own = jnp.where(row_keep[:, None], summed, 0.0).astype(jnp.bfloat16)
    with jax.named_scope("gather_attended"):
        attended_all = ring_gather(attended_near, "mp", shift_x, X)
    with jax.named_scope("gather_projection"):
        w_near = jnp.stack(ring_gather(w_far, "scene", shift_zl, ZL))

    own, attended_all, w_far = lax.optimization_barrier((own, attended_all, w_far))
    with jax.named_scope("weight_terms"):
        send, keep = weight_terms(place, attended_all, own)
    with jax.named_scope("sum_over_core"):
        pair = (keep + lax.ppermute(send, "scene", other_core())).astype(jnp.bfloat16)
    with jax.named_scope("gather_over_y"):
        block = gather(own, XY, y_groups())
    pair, w_near = lax.optimization_barrier((pair, w_near))
    with jax.named_scope("gather_projection"):
        w_other = lax.ppermute(w_near, "scene", other_core())
    with jax.named_scope("sum_over_z_lo"):
        parts = [
            lax.dynamic_index_in_dim(pair, (zl + k) & (ZL - 1), 0, keepdims=False)
            for k in range(ZL)
        ]
        near = sum_f32(ring_exchange(parts, "scene", shift_zl)).astype(jnp.bfloat16)

    near, block, w_other = lax.optimization_barrier((near, block, w_other))
    with jax.named_scope("sum_over_z_hi"):
        total = sum_f32(exchange(near, "scene", z_hi_groups()))
        d_wout = lax.ppermute(total, ("section", "scene", "mp"), swap_head_and_scene())
    with jax.named_scope("gather_over_x"):
        upstream = ring_gather(block, "mp", shift_x, X)

    with jax.named_scope("head_gradients"):
        d_attn = head_grad(place, upstream, w_near, w_other)
        d_queries, d_keys, d_values = attend_backward(
            queries, keys, values, d_attn, probs, weights, attended, scaling
        )
    return d_queries[None], d_keys[None], d_values[None], d_wout


def solution(mesh):
    heads = P("scene", None, XY)
    return jax.shard_map(
        shards,
        mesh=mesh,
        in_specs=(
            P("scene", XY, None, None),
            heads,
            heads,
            heads,
            P(XY, "scene"),
            P("scene", None, None),
            P("scene"),
        ),
        out_specs=(heads, heads, heads, P(XY, "scene")),
        check_vma=False,
    )
```

```python
import math

import jax
import jax.numpy as jnp
from jax import lax
from jax.experimental import pallas as pl
from jax.experimental.pallas import tpu as pltpu
from jax.sharding import PartitionSpec as P

HEAD_DIM = 128
XY = ("section", "mp")
X, YH, YL = 4, 4, 2
ZH, ZL, CORES = 4, 4, 2


def xy_index(x, y):
    return (y % YL) * (X * YH) + x * YH + y // YL


def scene_index(zh, zl, core):
    return (zh * ZL + zl) * CORES + core


def shift_x(k):
    return [(x * YH + y, ((x + k) % X) * YH + y) for x in range(X) for y in range(YH)]


def shift_zl(k):
    return [
        (scene_index(a, b, c), scene_index(a, (b + k) % ZL, c))
        for a in range(ZH)
        for b in range(ZL)
        for c in range(CORES)
    ]


def z_lo_groups():
    return [
        [scene_index(a, b, c) for b in range(ZL)] for a in range(ZH) for c in range(CORES)
    ]


def z_hi_groups():
    return [
        [scene_index(a, b, c) for a in range(ZH)] for b in range(ZL) for c in range(CORES)
    ]


def swap_x_zh():
    pairs = []
    for a in range(ZH):
        for rest in range(ZL * CORES):
            for x in range(X):
                for yh in range(YH):
                    here = ((a * ZL * CORES + rest) * X + x) * YH + yh
                    there = ((x * ZL * CORES + rest) * X + a) * YH + yh
                    pairs.append((here, there))
    return pairs


def other_core():
    return [(s, s ^ 1) for s in range(ZH * ZL * CORES)]


def y_groups():
    return [[xy_index(x, y) for y in range(YH * YL)] for x in range(X)]


def attend_forward(queries, keys, values, visible, scaling):
    scores = jnp.einsum("qd,kd->qk", queries, keys, preferred_element_type=jnp.float32) * scaling
    scores = jnp.where(visible, scores, -1e30)
    largest = jnp.max(scores, axis=-1, keepdims=True)
    exponent = jnp.exp(scores - largest)
    probs = exponent / jnp.sum(exponent, axis=-1, keepdims=True)
    weights = probs.astype(jnp.bfloat16)
    attended = jnp.einsum("qk,kd->qd", weights, values, preferred_element_type=jnp.float32)
    return probs, weights, attended


def attend_backward(queries, keys, values, grads, probs, weights, attended, scaling):
    delta = jnp.sum(grads.astype(jnp.float32) * attended, axis=-1)
    d_values = jnp.einsum("qk,qd->kd", weights, grads, preferred_element_type=jnp.float32)
    d_probs = jnp.einsum("qd,kd->qk", grads, values, preferred_element_type=jnp.float32)
    score_grads = (probs * (d_probs - delta[:, None])).astype(jnp.bfloat16)
    d_queries = scaling * jnp.einsum(
        "qk,kd->qd", score_grads, keys, preferred_element_type=jnp.float32
    )
    d_keys = scaling * jnp.einsum(
        "qk,qd->kd", score_grads, queries, preferred_element_type=jnp.float32
    )
    return [g.astype(jnp.bfloat16) for g in (d_queries, d_keys, d_values)]


def weight_terms_kernel(place_ref, block_ref, *refs):
    attended, (send_ref, keep_ref) = refs[:X], refs[X:]
    first = place_ref[0] == 0
    for k in range(X):
        head = (place_ref[1] + k) & (X - 1)
        term = lax.dot_general(
            attended[k][...],
            block_ref[...],
            (((0,), (0,)), ((), ())),
            preferred_element_type=jnp.float32,
        )
        for b in range(ZL):
            left = b * CORES * HEAD_DIM
            low = term[:, left : left + HEAD_DIM]
            high = term[:, left + HEAD_DIM : left + 2 * HEAD_DIM]
            send_ref[b, head] = jnp.where(first, high, low).astype(jnp.bfloat16)
            keep_ref[b, head] = jnp.where(first, low, high)


def weight_terms(place, block, attended):
    rows, width = block.shape
    shape = (ZL, X, HEAD_DIM, HEAD_DIM)
    vmem = pl.BlockSpec(memory_space=pltpu.VMEM)
    return pl.pallas_call(
        weight_terms_kernel,
        out_shape=(
            jax.ShapeDtypeStruct(shape, jnp.bfloat16),
            jax.ShapeDtypeStruct(shape, jnp.float32),
        ),
        in_specs=[pl.BlockSpec(memory_space=pltpu.SMEM)] + [vmem] * (1 + X),
        out_specs=(vmem, vmem),
        compiler_params=pltpu.CompilerParams(vmem_limit_bytes=24 << 20),
        cost_estimate=pl.CostEstimate(
            flops=2 * rows * width * X * HEAD_DIM,
            bytes_accessed=2 * rows * (width + X * HEAD_DIM) + 3 * width * X * HEAD_DIM,
            transcendentals=0,
        ),
        name="weight_terms",
    )(place, block, *attended)


def head_grad_kernel(place_ref, w_own_ref, w_other_ref, *refs):
    *blocks, out_ref = refs
    core, x, zl = [place_ref[i] for i in range(3)]
    total = jnp.zeros(out_ref.shape, jnp.float32)
    for k in range(X):
        far = (x + k) & (X - 1)
        for b in range(ZL):
            near = (b - zl) & (ZL - 1)
            left = b * CORES * HEAD_DIM
            own, other = w_own_ref[near, far], w_other_ref[near, far]
            first, second = jnp.where(core == 0, own, other), jnp.where(core == 0, other, own)
            for c, weight in enumerate((first, second)):
                total += lax.dot_general(
                    blocks[k][:, left + c * HEAD_DIM : left + (c + 1) * HEAD_DIM],
                    weight,
                    (((1,), (1,)), ((), ())),
                    preferred_element_type=jnp.float32,
                )
    out_ref[...] = total.astype(out_ref.dtype)


def head_grad(place, blocks, w_own, w_other):
    rows, width = blocks[0].shape
    vmem = pl.BlockSpec(memory_space=pltpu.VMEM)
    return pl.pallas_call(
        head_grad_kernel,
        out_shape=jax.ShapeDtypeStruct((rows, HEAD_DIM), jnp.bfloat16),
        in_specs=[pl.BlockSpec(memory_space=pltpu.SMEM)] + [vmem] * (2 + X),
        out_specs=vmem,
        compiler_params=pltpu.CompilerParams(vmem_limit_bytes=24 << 20),
        cost_estimate=pl.CostEstimate(
            flops=2 * rows * width * X * HEAD_DIM,
            bytes_accessed=2 * (rows + HEAD_DIM) * width * X,
            transcendentals=0,
        ),
        name="head_grad",
    )(place, w_own, w_other, *blocks)


def shift_right(number, size):
    return lax.shift_right_logical(number, size.bit_length() - 1)


def sum_f32(parts):
    total = parts[0].astype(jnp.float32)
    for k in range(1, len(parts)):
        total = total + parts[k].astype(jnp.float32)
    return total


def shards(dec_grad, agent_queries, map_keys, map_values, w_out, block_mask, agent_count):
    scaling = 1.0 / math.sqrt(HEAD_DIM)
    section, mp, scene = (lax.axis_index(name) for name in ("section", "mp", "scene"))
    x, y = shift_right(mp, YH), (mp & (YH - 1)) * YL + section
    zl = shift_right(scene, CORES) & (ZL - 1)
    core = scene & (CORES - 1)
    place = jnp.stack([core, x, zl])
    sample = dec_grad[0, 0]
    tokens, model = sample.shape
    width = model // X

    with jax.named_scope("sum_over_x"):
        pieces = [
            lax.dynamic_slice(sample, (0, ((x + k) & (X - 1)) * width), (tokens, width))
            for k in range(X)
        ]
        arrived = [lax.ppermute(pieces[k], "mp", shift_x(k)) for k in range(1, X)]
        partial = sum_f32([pieces[0]] + arrived).astype(jnp.bfloat16)

    with jax.named_scope("gather_projection"):
        w_spread = jnp.broadcast_to(w_out[None], (ZH, *w_out.shape))
        w_far = lax.all_to_all(w_spread, "scene", 0, 0, axis_index_groups=z_hi_groups())

    queries, keys, values = agent_queries[0], map_keys[0], map_values[0]
    mask_rows = block_mask[0]
    agent_block, map_block = tokens // mask_rows.shape[0], keys.shape[0] // mask_rows.shape[1]
    visible = jnp.repeat(jnp.repeat(mask_rows == 1, agent_block, axis=0), map_block, axis=1)
    probs, weights, attended = attend_forward(queries, keys, values, visible, scaling)
    attended_rounded = attended.astype(jnp.bfloat16)

    partial, w_far, attended_rounded = lax.optimization_barrier((partial, w_far, attended_rounded))
    with jax.named_scope("sum_over_y"):
        rows = tokens // (YH * YL)
        lines = lax.all_to_all(
            partial.reshape(YH * YL, rows, width), XY, 0, 0, axis_index_groups=y_groups()
        )
        summed = jnp.sum(lines.astype(jnp.float32), axis=0)
        row_keep = y * rows + jnp.arange(rows) < agent_count[0]
        own = jnp.where(row_keep[:, None], summed, 0.0).astype(jnp.bfloat16)
    with jax.named_scope("gather_attended"):
        attended_near = [attended_rounded] + [
            lax.ppermute(attended_rounded, "mp", shift_x(-k)) for k in range(1, X)
        ]

    own, attended_near = lax.optimization_barrier((own, attended_near))
    with jax.named_scope("gather_over_y"):
        spread = jnp.broadcast_to(own[None], (YH * YL, rows, width))
        block = lax.all_to_all(spread, XY, 0, 0, axis_index_groups=y_groups())
        block = block.reshape(tokens, width)
    with jax.named_scope("gather_projection"):
        w_near = jnp.stack(
            [w_far] + [lax.ppermute(w_far, "scene", shift_zl(-k)) for k in range(1, ZL)]
        )

    block, w_near = lax.optimization_barrier((block, w_near))
    with jax.named_scope("weight_terms"):
        send, keep = weight_terms(place, block, attended_near)

    with jax.named_scope("sum_over_core"):
        pair = sum_f32([keep, lax.ppermute(send, "scene", other_core())]).astype(jnp.bfloat16)

    with jax.named_scope("gather_projection"):
        w_other = lax.ppermute(w_near, "scene", other_core())

    with jax.named_scope("gather_over_x"):
        upstream = [block] + [lax.ppermute(block, "mp", shift_x(-k)) for k in range(1, X)]

    with jax.named_scope("sum_over_z_lo"):
        near = sum_f32(
            lax.all_to_all(pair, "scene", 0, 0, axis_index_groups=z_lo_groups())
        ).astype(jnp.bfloat16)

    near, upstream, w_other = lax.optimization_barrier((near, upstream, w_other))
    with jax.named_scope("sum_over_z_hi"):
        summed_block = sum_f32(
            lax.all_to_all(near, "scene", 0, 0, axis_index_groups=z_hi_groups())
        )
        d_wout = lax.ppermute(summed_block, ("scene", "mp"), swap_x_zh())

    with jax.named_scope("head_gradients"):
        d_attn = head_grad(place, upstream, w_near, w_other)
        d_queries, d_keys, d_values = attend_backward(
            queries, keys, values, d_attn, probs, weights, attended, scaling
        )
    return d_queries[None], d_keys[None], d_values[None], d_wout


def solution(mesh):
    heads = P("scene", None, XY)
    return jax.shard_map(
        shards,
        mesh=mesh,
        in_specs=(
            P("scene", XY, None, None),
            heads,
            heads,
            heads,
            P(XY, "scene"),
            P("scene", None, None),
            P("scene"),
        ),
        out_specs=(heads, heads, heads, P(XY, "scene")),
        check_vma=False,
    )
```

```python
import math

import jax
import jax.numpy as jnp
from jax import lax
from jax.experimental import pallas as pl
from jax.experimental.pallas import tpu as pltpu
from jax.sharding import PartitionSpec as P

HEAD_DIM = 128
XY = ("section", "mp")
X, YH, YL = 4, 4, 2
ZH, ZL, CORES = 4, 4, 2


def xy_index(x, y):
    return (y % YL) * (X * YH) + x * YH + y // YL


def scene_index(zh, zl, core):
    return (zh * ZL + zl) * CORES + core


def shift_x(k):
    return [(x * YH + y, ((x + k) % X) * YH + y) for x in range(X) for y in range(YH)]


def shift_zl(k):
    return [
        (scene_index(a, b, c), scene_index(a, (b + k) % ZL, c))
        for a in range(ZH)
        for b in range(ZL)
        for c in range(CORES)
    ]


def shift_zh(k):
    return [
        (scene_index(a, b, c), scene_index((a + k) % ZH, b, c))
        for a in range(ZH)
        for b in range(ZL)
        for c in range(CORES)
    ]


def z_lo_groups():
    return [
        [scene_index(a, b, c) for b in range(ZL)] for a in range(ZH) for c in range(CORES)
    ]


def z_hi_groups():
    return [
        [scene_index(a, b, c) for a in range(ZH)] for b in range(ZL) for c in range(CORES)
    ]


def swap_x_zh():
    pairs = []
    for a in range(ZH):
        for rest in range(ZL * CORES):
            for x in range(X):
                for yh in range(YH):
                    here = ((a * ZL * CORES + rest) * X + x) * YH + yh
                    there = ((x * ZL * CORES + rest) * X + a) * YH + yh
                    pairs.append((here, there))
    return pairs


def other_core():
    return [(s, s ^ 1) for s in range(ZH * ZL * CORES)]


def y_groups():
    return [[xy_index(x, y) for y in range(YH * YL)] for x in range(X)]


def attend_forward(queries, keys, values, visible, scaling):
    scores = jnp.einsum("qd,kd->qk", queries, keys, preferred_element_type=jnp.float32) * scaling
    scores = jnp.where(visible, scores, -1e30)
    largest = jnp.max(scores, axis=-1, keepdims=True)
    exponent = jnp.exp(scores - largest)
    probs = exponent / jnp.sum(exponent, axis=-1, keepdims=True)
    weights = probs.astype(jnp.bfloat16)
    attended = jnp.einsum("qk,kd->qd", weights, values, preferred_element_type=jnp.float32)
    return probs, weights, attended


def attend_backward(queries, keys, values, grads, probs, weights, attended, scaling):
    delta = jnp.sum(grads.astype(jnp.float32) * attended, axis=-1)
    d_values = jnp.einsum("qk,qd->kd", weights, grads, preferred_element_type=jnp.float32)
    d_probs = jnp.einsum("qd,kd->qk", grads, values, preferred_element_type=jnp.float32)
    score_grads = (probs * (d_probs - delta[:, None])).astype(jnp.bfloat16)
    d_queries = scaling * jnp.einsum(
        "qk,kd->qd", score_grads, keys, preferred_element_type=jnp.float32
    )
    d_keys = scaling * jnp.einsum(
        "qk,qd->kd", score_grads, queries, preferred_element_type=jnp.float32
    )
    return [g.astype(jnp.bfloat16) for g in (d_queries, d_keys, d_values)]


def add_own_kernel(x_ref, own_ref, *refs):
    *part_refs, out_ref = refs
    total = own_ref[...].astype(jnp.float32)
    for part_ref in part_refs:
        total += part_ref[...].astype(jnp.float32)
    out_ref[...] = total.astype(out_ref.dtype)


def add_own(x, sample, arrived):
    rows, width = arrived[0].shape
    whole = pl.BlockSpec((rows, width), lambda i, x: (0, 0))
    return pl.pallas_call(
        add_own_kernel,
        out_shape=jax.ShapeDtypeStruct((rows, width), jnp.bfloat16),
        grid_spec=pltpu.PrefetchScalarGridSpec(
            num_scalar_prefetch=1,
            grid=(1,),
            in_specs=[pl.BlockSpec((rows, width), lambda i, x: (0, x[0]))] + [whole] * (X - 1),
            out_specs=whole,
        ),
        compiler_params=pltpu.CompilerParams(vmem_limit_bytes=16 << 20),
        cost_estimate=pl.CostEstimate(
            flops=rows * width * X, bytes_accessed=2 * rows * width * (X + 1), transcendentals=0
        ),
        name="add_own",
    )(x.reshape(1), sample, *arrived)


def weight_terms_kernel(place_ref, block_ref, *refs):
    attended, (send_ref, keep_ref) = refs[:X], refs[X:]
    first = place_ref[0] == 0
    for k in range(X):
        head = (place_ref[1] + k) & (X - 1)
        term = lax.dot_general(
            attended[k][...],
            block_ref[...],
            (((0,), (0,)), ((), ())),
            preferred_element_type=jnp.float32,
        )
        for b in range(ZL):
            left = b * CORES * HEAD_DIM
            low = term[:, left : left + HEAD_DIM]
            high = term[:, left + HEAD_DIM : left + 2 * HEAD_DIM]
            send_ref[b, head] = jnp.where(first, high, low).astype(jnp.bfloat16)
            keep_ref[b, head] = jnp.where(first, low, high)


def weight_terms(place, block, attended):
    rows, width = block.shape
    shape = (ZL, X, HEAD_DIM, HEAD_DIM)
    vmem = pl.BlockSpec(memory_space=pltpu.VMEM)
    return pl.pallas_call(
        weight_terms_kernel,
        out_shape=(
            jax.ShapeDtypeStruct(shape, jnp.bfloat16),
            jax.ShapeDtypeStruct(shape, jnp.float32),
        ),
        in_specs=[pl.BlockSpec(memory_space=pltpu.SMEM)] + [vmem] * (1 + X),
        out_specs=(vmem, vmem),
        compiler_params=pltpu.CompilerParams(vmem_limit_bytes=24 << 20),
        cost_estimate=pl.CostEstimate(
            flops=2 * rows * width * X * HEAD_DIM,
            bytes_accessed=2 * rows * (width + X * HEAD_DIM) + 3 * width * X * HEAD_DIM,
            transcendentals=0,
        ),
        name="weight_terms",
    )(place, block, *attended)


def head_grad_kernel(place_ref, w_own_ref, w_other_ref, *refs):
    *blocks, out_ref = refs
    core, x, zl, zh = [place_ref[i] for i in range(4)]
    total = jnp.zeros(out_ref.shape, jnp.float32)
    for k in range(X):
        far = (x + k - zh) & (ZH - 1)
        for b in range(ZL):
            near = (b - zl) & (ZL - 1)
            left = b * CORES * HEAD_DIM
            own, other = w_own_ref[near, far], w_other_ref[near, far]
            first, second = jnp.where(core == 0, own, other), jnp.where(core == 0, other, own)
            for c, weight in enumerate((first, second)):
                total += lax.dot_general(
                    blocks[k][:, left + c * HEAD_DIM : left + (c + 1) * HEAD_DIM],
                    weight,
                    (((1,), (1,)), ((), ())),
                    preferred_element_type=jnp.float32,
                )
    out_ref[...] = total.astype(out_ref.dtype)


def head_grad(place, blocks, w_own, w_other):
    rows, width = blocks[0].shape
    vmem = pl.BlockSpec(memory_space=pltpu.VMEM)
    return pl.pallas_call(
        head_grad_kernel,
        out_shape=jax.ShapeDtypeStruct((rows, HEAD_DIM), jnp.bfloat16),
        in_specs=[pl.BlockSpec(memory_space=pltpu.SMEM)] + [vmem] * (2 + X),
        out_specs=vmem,
        compiler_params=pltpu.CompilerParams(vmem_limit_bytes=24 << 20),
        cost_estimate=pl.CostEstimate(
            flops=2 * rows * width * X * HEAD_DIM,
            bytes_accessed=2 * (rows + HEAD_DIM) * width * X,
            transcendentals=0,
        ),
        name="head_grad",
    )(place, w_own, w_other, *blocks)


def shift_right(number, size):
    return lax.shift_right_logical(number, size.bit_length() - 1)


def sum_f32(parts):
    total = parts[0].astype(jnp.float32)
    for k in range(1, len(parts)):
        total = total + parts[k].astype(jnp.float32)
    return total


def shards(dec_grad, agent_queries, map_keys, map_values, w_out, block_mask, agent_count):
    scaling = 1.0 / math.sqrt(HEAD_DIM)
    section, mp, scene = (lax.axis_index(name) for name in ("section", "mp", "scene"))
    x, y = shift_right(mp, YH), (mp & (YH - 1)) * YL + section
    zh, zl = shift_right(scene, ZL * CORES), shift_right(scene, CORES) & (ZL - 1)
    core = scene & (CORES - 1)
    place = jnp.stack([core, x, zl, zh])
    sample = dec_grad[0, 0]
    tokens, model = sample.shape
    width = model // X

    with jax.named_scope("sum_over_x"):
        pieces = [
            lax.dynamic_slice(sample, (0, ((x + k) & (X - 1)) * width), (tokens, width))
            for k in range(1, X)
        ]
        arrived = [lax.ppermute(piece, "mp", shift_x(k + 1)) for k, piece in enumerate(pieces)]
        partial = add_own(x, sample, arrived)

    with jax.named_scope("gather_projection"):
        w_rows = [w_out] + [lax.ppermute(w_out, "scene", shift_zh(-k)) for k in range(1, ZH)]

    queries, keys, values = agent_queries[0], map_keys[0], map_values[0]
    mask_rows = block_mask[0]
    agent_block, map_block = tokens // mask_rows.shape[0], keys.shape[0] // mask_rows.shape[1]
    visible = jnp.repeat(jnp.repeat(mask_rows == 1, agent_block, axis=0), map_block, axis=1)
    probs, weights, attended = attend_forward(queries, keys, values, visible, scaling)
    attended_rounded = attended.astype(jnp.bfloat16)

    partial, w_rows[1], attended_rounded = lax.optimization_barrier(
        (partial, w_rows[1], attended_rounded)
    )
    with jax.named_scope("sum_over_y"):
        rows = tokens // (YH * YL)
        lines = lax.all_to_all(
            partial.reshape(YH * YL, rows, width), XY, 0, 0, axis_index_groups=y_groups()
        )
        summed = jnp.sum(lines.astype(jnp.float32), axis=0)
        row_keep = y * rows + jnp.arange(rows) < agent_count[0]
        own = jnp.where(row_keep[:, None], summed, 0.0).astype(jnp.bfloat16)
    with jax.named_scope("gather_attended"):
        attended_near = [attended_rounded] + [
            lax.ppermute(attended_rounded, "mp", shift_x(-k)) for k in range(1, X)
        ]

    own, attended_near, w_rows = lax.optimization_barrier((own, attended_near, w_rows))
    w_far = jnp.stack(w_rows)
    with jax.named_scope("gather_over_y"):
        spread = jnp.broadcast_to(own[None], (YH * YL, rows, width))
        block = lax.all_to_all(spread, XY, 0, 0, axis_index_groups=y_groups())
        block = block.reshape(tokens, width)
    with jax.named_scope("gather_projection"):
        w_near = jnp.stack(
            [w_far] + [lax.ppermute(w_far, "scene", shift_zl(-k)) for k in range(1, ZL)]
        )

    block, w_near = lax.optimization_barrier((block, w_near))
    with jax.named_scope("weight_terms"):
        send, keep = weight_terms(place, block, attended_near)

    with jax.named_scope("sum_over_core"):
        pair = sum_f32([keep, lax.ppermute(send, "scene", other_core())]).astype(jnp.bfloat16)

    with jax.named_scope("gather_projection"):
        w_other = lax.ppermute(w_near, "scene", other_core())

    with jax.named_scope("gather_over_x"):
        upstream = [block] + [lax.ppermute(block, "mp", shift_x(-k)) for k in range(1, X)]

    with jax.named_scope("sum_over_z_lo"):
        near = sum_f32(
            lax.all_to_all(pair, "scene", 0, 0, axis_index_groups=z_lo_groups())
        ).astype(jnp.bfloat16)

    with jax.named_scope("sum_over_z_hi"):
        summed_block = sum_f32(
            lax.all_to_all(near, "scene", 0, 0, axis_index_groups=z_hi_groups())
        )
        d_wout = lax.ppermute(summed_block, ("scene", "mp"), swap_x_zh())

    with jax.named_scope("head_gradients"):
        upstream, w_other, _ = lax.optimization_barrier((upstream, w_other, near))
        d_attn = head_grad(place, upstream, w_near, w_other)
        d_queries, d_keys, d_values = attend_backward(
            queries, keys, values, d_attn, probs, weights, attended, scaling
        )
    return d_queries[None], d_keys[None], d_values[None], d_wout


def solution(mesh):
    heads = P("scene", None, XY)
    return jax.shard_map(
        shards,
        mesh=mesh,
        in_specs=(
            P("scene", XY, None, None),
            heads,
            heads,
            heads,
            P(XY, "scene"),
            P("scene", None, None),
            P("scene"),
        ),
        out_specs=(heads, heads, heads, P(XY, "scene")),
        check_vma=False,
    )
```

```python
import math

import jax
import jax.numpy as jnp
from jax import lax
from jax.experimental import pallas as pl
from jax.experimental.pallas import tpu as pltpu
from jax.sharding import PartitionSpec as P

HEAD_DIM = 128
XY = ("section", "mp")
X, YH, YL = 4, 4, 2
ZH, ZL, CORES = 4, 4, 2


def xy_index(x, y):
    return (y % YL) * (X * YH) + x * YH + y // YL


def scene_index(zh, zl, core):
    return (zh * ZL + zl) * CORES + core


def shift_x(k):
    return [(x * YH + y, ((x + k) % X) * YH + y) for x in range(X) for y in range(YH)]


def shift_zl(k):
    return [
        (scene_index(a, b, c), scene_index(a, (b + k) % ZL, c))
        for a in range(ZH)
        for b in range(ZL)
        for c in range(CORES)
    ]


def z_lo_groups():
    return [
        [scene_index(a, b, c) for b in range(ZL)] for a in range(ZH) for c in range(CORES)
    ]


def z_hi_groups():
    return [
        [scene_index(a, b, c) for a in range(ZH)] for b in range(ZL) for c in range(CORES)
    ]


def swap_x_zh():
    pairs = []
    for a in range(ZH):
        for rest in range(ZL * CORES):
            for x in range(X):
                for yh in range(YH):
                    here = ((a * ZL * CORES + rest) * X + x) * YH + yh
                    there = ((x * ZL * CORES + rest) * X + a) * YH + yh
                    pairs.append((here, there))
    return pairs


def other_core():
    return [(s, s ^ 1) for s in range(ZH * ZL * CORES)]


def y_groups():
    return [[xy_index(x, y) for y in range(YH * YL)] for x in range(X)]


def attend_forward(queries, keys, values, visible, scaling):
    scores = jnp.einsum("qd,kd->qk", queries, keys, preferred_element_type=jnp.float32) * scaling
    scores = jnp.where(visible, scores, -1e30)
    largest = jnp.max(scores, axis=-1, keepdims=True)
    exponent = jnp.exp(scores - largest)
    probs = exponent / jnp.sum(exponent, axis=-1, keepdims=True)
    weights = probs.astype(jnp.bfloat16)
    attended = jnp.einsum("qk,kd->qd", weights, values, preferred_element_type=jnp.float32)
    return probs, weights, attended


def attend_backward(queries, keys, values, grads, probs, weights, attended, scaling):
    delta = jnp.sum(grads.astype(jnp.float32) * attended, axis=-1)
    d_values = jnp.einsum("qk,qd->kd", weights, grads, preferred_element_type=jnp.float32)
    d_probs = jnp.einsum("qd,kd->qk", grads, values, preferred_element_type=jnp.float32)
    score_grads = (probs * (d_probs - delta[:, None])).astype(jnp.bfloat16)
    d_queries = scaling * jnp.einsum(
        "qk,kd->qd", score_grads, keys, preferred_element_type=jnp.float32
    )
    d_keys = scaling * jnp.einsum(
        "qk,qd->kd", score_grads, queries, preferred_element_type=jnp.float32
    )
    return [g.astype(jnp.bfloat16) for g in (d_queries, d_keys, d_values)]


def add_own_kernel(x_ref, own_ref, *refs):
    *part_refs, out_ref = refs
    total = own_ref[...].astype(jnp.float32)
    for part_ref in part_refs:
        total += part_ref[...].astype(jnp.float32)
    out_ref[...] = total.astype(out_ref.dtype)


def add_own(x, sample, arrived):
    rows, width = arrived[0].shape
    whole = pl.BlockSpec((rows, width), lambda i, x: (0, 0))
    return pl.pallas_call(
        add_own_kernel,
        out_shape=jax.ShapeDtypeStruct((rows, width), jnp.bfloat16),
        grid_spec=pltpu.PrefetchScalarGridSpec(
            num_scalar_prefetch=1,
            grid=(1,),
            in_specs=[pl.BlockSpec((rows, width), lambda i, x: (0, x[0]))] + [whole] * (X - 1),
            out_specs=whole,
        ),
        compiler_params=pltpu.CompilerParams(vmem_limit_bytes=16 << 20),
        cost_estimate=pl.CostEstimate(
            flops=rows * width * X, bytes_accessed=2 * rows * width * (X + 1), transcendentals=0
        ),
        name="add_own",
    )(x.reshape(1), sample, *arrived)


def weight_terms_kernel(place_ref, block_ref, *refs):
    attended, (send_ref, keep_ref) = refs[:X], refs[X:]
    first = place_ref[0] == 0
    for k in range(X):
        head = (place_ref[1] + k) & (X - 1)
        term = lax.dot_general(
            attended[k][...],
            block_ref[...],
            (((0,), (0,)), ((), ())),
            preferred_element_type=jnp.float32,
        )
        for b in range(ZL):
            left = b * CORES * HEAD_DIM
            low = term[:, left : left + HEAD_DIM]
            high = term[:, left + HEAD_DIM : left + 2 * HEAD_DIM]
            send_ref[b, head] = jnp.where(first, high, low).astype(jnp.bfloat16)
            keep_ref[b, head] = jnp.where(first, low, high)


def weight_terms(place, block, attended):
    rows, width = block.shape
    shape = (ZL, X, HEAD_DIM, HEAD_DIM)
    vmem = pl.BlockSpec(memory_space=pltpu.VMEM)
    return pl.pallas_call(
        weight_terms_kernel,
        out_shape=(
            jax.ShapeDtypeStruct(shape, jnp.bfloat16),
            jax.ShapeDtypeStruct(shape, jnp.float32),
        ),
        in_specs=[pl.BlockSpec(memory_space=pltpu.SMEM)] + [vmem] * (1 + X),
        out_specs=(vmem, vmem),
        compiler_params=pltpu.CompilerParams(vmem_limit_bytes=24 << 20),
        cost_estimate=pl.CostEstimate(
            flops=2 * rows * width * X * HEAD_DIM,
            bytes_accessed=2 * rows * (width + X * HEAD_DIM) + 3 * width * X * HEAD_DIM,
            transcendentals=0,
        ),
        name="weight_terms",
    )(place, block, *attended)


def head_grad_kernel(place_ref, w_own_ref, w_other_ref, *refs):
    *blocks, out_ref = refs
    core, x, zl = [place_ref[i] for i in range(3)]
    total = jnp.zeros(out_ref.shape, jnp.float32)
    for k in range(X):
        far = (x + k) & (X - 1)
        for b in range(ZL):
            near = (b - zl) & (ZL - 1)
            left = b * CORES * HEAD_DIM
            own, other = w_own_ref[near, far], w_other_ref[near, far]
            first, second = jnp.where(core == 0, own, other), jnp.where(core == 0, other, own)
            for c, weight in enumerate((first, second)):
                total += lax.dot_general(
                    blocks[k][:, left + c * HEAD_DIM : left + (c + 1) * HEAD_DIM],
                    weight,
                    (((1,), (1,)), ((), ())),
                    preferred_element_type=jnp.float32,
                )
    out_ref[...] = total.astype(out_ref.dtype)


def head_grad(place, blocks, w_own, w_other):
    rows, width = blocks[0].shape
    vmem = pl.BlockSpec(memory_space=pltpu.VMEM)
    return pl.pallas_call(
        head_grad_kernel,
        out_shape=jax.ShapeDtypeStruct((rows, HEAD_DIM), jnp.bfloat16),
        in_specs=[pl.BlockSpec(memory_space=pltpu.SMEM)] + [vmem] * (2 + X),
        out_specs=vmem,
        compiler_params=pltpu.CompilerParams(vmem_limit_bytes=24 << 20),
        cost_estimate=pl.CostEstimate(
            flops=2 * rows * width * X * HEAD_DIM,
            bytes_accessed=2 * (rows + HEAD_DIM) * width * X,
            transcendentals=0,
        ),
        name="head_grad",
    )(place, w_own, w_other, *blocks)


def shift_right(number, size):
    return lax.shift_right_logical(number, size.bit_length() - 1)


def sum_f32(parts):
    total = parts[0].astype(jnp.float32)
    for k in range(1, len(parts)):
        total = total + parts[k].astype(jnp.float32)
    return total


def shards(dec_grad, agent_queries, map_keys, map_values, w_out, block_mask, agent_count):
    scaling = 1.0 / math.sqrt(HEAD_DIM)
    section, mp, scene = (lax.axis_index(name) for name in ("section", "mp", "scene"))
    x, y = shift_right(mp, YH), (mp & (YH - 1)) * YL + section
    zl = shift_right(scene, CORES) & (ZL - 1)
    core = scene & (CORES - 1)
    place = jnp.stack([core, x, zl])
    sample = dec_grad[0, 0]
    tokens, model = sample.shape
    width = model // X

    with jax.named_scope("sum_over_x"):
        pieces = [
            lax.dynamic_slice(sample, (0, ((x + k) & (X - 1)) * width), (tokens, width))
            for k in range(1, X)
        ]
        arrived = [lax.ppermute(piece, "mp", shift_x(k + 1)) for k, piece in enumerate(pieces)]
        partial = add_own(x, sample, arrived)

    with jax.named_scope("gather_projection"):
        w_spread = jnp.broadcast_to(w_out[None], (ZH, *w_out.shape))
        w_far = lax.all_to_all(w_spread, "scene", 0, 0, axis_index_groups=z_hi_groups())

    queries, keys, values = agent_queries[0], map_keys[0], map_values[0]
    mask_rows = block_mask[0]
    agent_block, map_block = tokens // mask_rows.shape[0], keys.shape[0] // mask_rows.shape[1]
    visible = jnp.repeat(jnp.repeat(mask_rows == 1, agent_block, axis=0), map_block, axis=1)
    probs, weights, attended = attend_forward(queries, keys, values, visible, scaling)
    attended_rounded = attended.astype(jnp.bfloat16)

    partial, w_far, attended_rounded = lax.optimization_barrier((partial, w_far, attended_rounded))
    with jax.named_scope("sum_over_y"):
        rows = tokens // (YH * YL)
        lines = lax.all_to_all(
            partial.reshape(YH * YL, rows, width), XY, 0, 0, axis_index_groups=y_groups()
        )
        summed = jnp.sum(lines.astype(jnp.float32), axis=0)
        row_keep = y * rows + jnp.arange(rows) < agent_count[0]
        own = jnp.where(row_keep[:, None], summed, 0.0).astype(jnp.bfloat16)
    with jax.named_scope("gather_attended"):
        attended_near = [attended_rounded] + [
            lax.ppermute(attended_rounded, "mp", shift_x(-k)) for k in range(1, X)
        ]

    own, attended_near = lax.optimization_barrier((own, attended_near))
    with jax.named_scope("gather_over_y"):
        spread = jnp.broadcast_to(own[None], (YH * YL, rows, width))
        block = lax.all_to_all(spread, XY, 0, 0, axis_index_groups=y_groups())
        block = block.reshape(tokens, width)
    with jax.named_scope("gather_projection"):
        w_near = jnp.stack(
            [w_far] + [lax.ppermute(w_far, "scene", shift_zl(-k)) for k in range(1, ZL)]
        )

    block, w_near = lax.optimization_barrier((block, w_near))
    with jax.named_scope("weight_terms"):
        send, keep = weight_terms(place, block, attended_near)

    with jax.named_scope("sum_over_core"):
        pair = sum_f32([keep, lax.ppermute(send, "scene", other_core())]).astype(jnp.bfloat16)

    with jax.named_scope("gather_projection"):
        w_other = lax.ppermute(w_near, "scene", other_core())

    with jax.named_scope("gather_over_x"):
        upstream = [block] + [lax.ppermute(block, "mp", shift_x(-k)) for k in range(1, X)]

    with jax.named_scope("sum_over_z_lo"):
        near = sum_f32(
            lax.all_to_all(pair, "scene", 0, 0, axis_index_groups=z_lo_groups())
        ).astype(jnp.bfloat16)

    with jax.named_scope("sum_over_z_hi"):
        summed_block = sum_f32(
            lax.all_to_all(near, "scene", 0, 0, axis_index_groups=z_hi_groups())
        )
        d_wout = lax.ppermute(summed_block, ("scene", "mp"), swap_x_zh())

    with jax.named_scope("head_gradients"):
        upstream, w_other, _ = lax.optimization_barrier((upstream, w_other, near))
        d_attn = head_grad(place, upstream, w_near, w_other)
        d_queries, d_keys, d_values = attend_backward(
            queries, keys, values, d_attn, probs, weights, attended, scaling
        )
    return d_queries[None], d_keys[None], d_values[None], d_wout


def solution(mesh):
    heads = P("scene", None, XY)
    return jax.shard_map(
        shards,
        mesh=mesh,
        in_specs=(
            P("scene", XY, None, None),
            heads,
            heads,
            heads,
            P(XY, "scene"),
            P("scene", None, None),
            P("scene"),
        ),
        out_specs=(heads, heads, heads, P(XY, "scene")),
        check_vma=False,
    )
```

```python
import math

import jax
import jax.numpy as jnp
from jax import lax
from jax.experimental import pallas as pl
from jax.experimental.pallas import tpu as pltpu
from jax.sharding import PartitionSpec as P

HEAD_DIM = 128
XY = ("section", "mp")
X, YH, YL = 4, 4, 2
ZH, ZL, CORES = 4, 4, 2


def xy_index(x, y):
    return (y % YL) * (X * YH) + x * YH + y // YL


def scene_index(zh, zl, core):
    return (zh * ZL + zl) * CORES + core


def shift_x(k):
    return [(x * YH + y, ((x + k) % X) * YH + y) for x in range(X) for y in range(YH)]


def shift_zl(k):
    return [
        (scene_index(a, b, c), scene_index(a, (b + k) % ZL, c))
        for a in range(ZH)
        for b in range(ZL)
        for c in range(CORES)
    ]


def x_groups():
    return [[x * YH + y for x in range(X)] for y in range(YH)]


def z_hi_groups():
    return [
        [scene_index(a, b, c) for a in range(ZH)] for b in range(ZL) for c in range(CORES)
    ]


def to_owner(k):
    pairs = []
    for a in range(ZH):
        for rest in range(ZL * CORES):
            for x in range(X):
                for yh in range(YH):
                    here = ((a * ZL * CORES + rest) * X + x) * YH + yh
                    there = ((x * ZL * CORES + rest) * X + (a + k) % X) * YH + yh
                    pairs.append((here, there))
    return pairs


def other_core():
    return [(s, s ^ 1) for s in range(ZH * ZL * CORES)]


def y_groups():
    return [[xy_index(x, y) for y in range(YH * YL)] for x in range(X)]


def attend_forward(queries, keys, values, visible, scaling):
    scores = jnp.einsum("qd,kd->qk", queries, keys, preferred_element_type=jnp.float32) * scaling
    scores = jnp.where(visible, scores, -1e30)
    largest = jnp.max(scores, axis=-1, keepdims=True)
    exponent = jnp.exp(scores - largest)
    probs = exponent / jnp.sum(exponent, axis=-1, keepdims=True)
    weights = probs.astype(jnp.bfloat16)
    attended = jnp.einsum("qk,kd->qd", weights, values, preferred_element_type=jnp.float32)
    return probs, weights, attended


def attend_backward(queries, keys, values, grads, probs, weights, attended, scaling):
    delta = jnp.sum(grads.astype(jnp.float32) * attended, axis=-1)
    d_values = jnp.einsum("qk,qd->kd", weights, grads, preferred_element_type=jnp.float32)
    d_probs = jnp.einsum("qd,kd->qk", grads, values, preferred_element_type=jnp.float32)
    score_grads = (probs * (d_probs - delta[:, None])).astype(jnp.bfloat16)
    d_queries = scaling * jnp.einsum(
        "qk,kd->qd", score_grads, keys, preferred_element_type=jnp.float32
    )
    d_keys = scaling * jnp.einsum(
        "qk,qd->kd", score_grads, queries, preferred_element_type=jnp.float32
    )
    return [g.astype(jnp.bfloat16) for g in (d_queries, d_keys, d_values)]


def add_own_kernel(x_ref, own_ref, *refs):
    *part_refs, out_ref = refs
    total = own_ref[...].astype(jnp.float32)
    for part_ref in part_refs:
        total += part_ref[...].astype(jnp.float32)
    out_ref[...] = total.astype(out_ref.dtype)


def add_own(x, sample, arrived):
    rows, width = arrived[0].shape
    whole = pl.BlockSpec((rows, width), lambda i, x: (0, 0))
    return pl.pallas_call(
        add_own_kernel,
        out_shape=jax.ShapeDtypeStruct((rows, width), jnp.bfloat16),
        grid_spec=pltpu.PrefetchScalarGridSpec(
            num_scalar_prefetch=1,
            grid=(1,),
            in_specs=[pl.BlockSpec((rows, width), lambda i, x: (0, x[0]))] + [whole] * (X - 1),
            out_specs=whole,
        ),
        compiler_params=pltpu.CompilerParams(vmem_limit_bytes=16 << 20),
        cost_estimate=pl.CostEstimate(
            flops=rows * width * X, bytes_accessed=2 * rows * width * (X + 1), transcendentals=0
        ),
        name="add_own",
    )(x.reshape(1), sample, *arrived)


def weight_terms_kernel(place_ref, block_ref, *refs):
    attended, (send_ref, keep_ref) = refs[:X], refs[X:]
    first = place_ref[0] == 0
    for k in range(X):
        head = (place_ref[1] + k) & (X - 1)
        term = lax.dot_general(
            attended[k][...],
            block_ref[...],
            (((0,), (0,)), ((), ())),
            preferred_element_type=jnp.float32,
        )
        for b in range(ZL):
            left = b * CORES * HEAD_DIM
            low = term[:, left : left + HEAD_DIM]
            high = term[:, left + HEAD_DIM : left + 2 * HEAD_DIM]
            send_ref[b, head] = jnp.where(first, high, low).astype(jnp.bfloat16)
            keep_ref[b, head] = jnp.where(first, low, high)


def weight_terms(place, block, attended):
    rows, width = block.shape
    shape = (ZL, X, HEAD_DIM, HEAD_DIM)
    vmem = pl.BlockSpec(memory_space=pltpu.VMEM)
    return pl.pallas_call(
        weight_terms_kernel,
        out_shape=(
            jax.ShapeDtypeStruct(shape, jnp.bfloat16),
            jax.ShapeDtypeStruct(shape, jnp.float32),
        ),
        in_specs=[pl.BlockSpec(memory_space=pltpu.SMEM)] + [vmem] * (1 + X),
        out_specs=(vmem, vmem),
        compiler_params=pltpu.CompilerParams(vmem_limit_bytes=24 << 20),
        cost_estimate=pl.CostEstimate(
            flops=2 * rows * width * X * HEAD_DIM,
            bytes_accessed=2 * rows * (width + X * HEAD_DIM) + 3 * width * X * HEAD_DIM,
            transcendentals=0,
        ),
        name="weight_terms",
    )(place, block, *attended)


def head_grad_kernel(place_ref, w_own_ref, w_other_ref, upstream_ref, out_ref):
    core, zl = place_ref[0], place_ref[2]
    total = jnp.zeros(out_ref.shape, jnp.float32)
    for a in range(X):
        for b in range(ZL):
            near = (b - zl) & (ZL - 1)
            left = b * CORES * HEAD_DIM
            own, other = w_own_ref[near, a], w_other_ref[near, a]
            first, second = jnp.where(core == 0, own, other), jnp.where(core == 0, other, own)
            for c, weight in enumerate((first, second)):
                total += lax.dot_general(
                    upstream_ref[a, :, left + c * HEAD_DIM : left + (c + 1) * HEAD_DIM],
                    weight,
                    (((1,), (1,)), ((), ())),
                    preferred_element_type=jnp.float32,
                )
    out_ref[...] = total.astype(out_ref.dtype)


def head_grad(place, upstream, w_own, w_other):
    _, rows, width = upstream.shape
    vmem = pl.BlockSpec(memory_space=pltpu.VMEM)
    return pl.pallas_call(
        head_grad_kernel,
        out_shape=jax.ShapeDtypeStruct((rows, HEAD_DIM), jnp.bfloat16),
        in_specs=[pl.BlockSpec(memory_space=pltpu.SMEM)] + [vmem] * 3,
        out_specs=vmem,
        compiler_params=pltpu.CompilerParams(vmem_limit_bytes=24 << 20),
        cost_estimate=pl.CostEstimate(
            flops=2 * rows * width * X * HEAD_DIM,
            bytes_accessed=2 * (rows + HEAD_DIM) * width * X,
            transcendentals=0,
        ),
        name="head_grad",
    )(place, w_own, w_other, upstream)


def shift_right(number, size):
    return lax.shift_right_logical(number, size.bit_length() - 1)


def sum_f32(parts):
    total = parts[0].astype(jnp.float32)
    for k in range(1, len(parts)):
        total = total + parts[k].astype(jnp.float32)
    return total


def shards(dec_grad, agent_queries, map_keys, map_values, w_out, block_mask, agent_count):
    scaling = 1.0 / math.sqrt(HEAD_DIM)
    section, mp, scene = (lax.axis_index(name) for name in ("section", "mp", "scene"))
    x, y = shift_right(mp, YH), (mp & (YH - 1)) * YL + section
    zh, zl = shift_right(scene, ZL * CORES), shift_right(scene, CORES) & (ZL - 1)
    core = scene & (CORES - 1)
    place = jnp.stack([core, x, zl])
    sample = dec_grad[0, 0]
    tokens, model = sample.shape
    width = model // X

    with jax.named_scope("sum_over_x"):
        pieces = [
            lax.dynamic_slice(sample, (0, ((x + k) & (X - 1)) * width), (tokens, width))
            for k in range(1, X)
        ]
        arrived = [lax.ppermute(piece, "mp", shift_x(k + 1)) for k, piece in enumerate(pieces)]
        partial = add_own(x, sample, arrived)

    with jax.named_scope("gather_projection"):
        w_spread = jnp.broadcast_to(w_out[None], (ZH, *w_out.shape))
        w_far = lax.all_to_all(w_spread, "scene", 0, 0, axis_index_groups=z_hi_groups())

    queries, keys, values = agent_queries[0], map_keys[0], map_values[0]
    mask_rows = block_mask[0]
    agent_block, map_block = tokens // mask_rows.shape[0], keys.shape[0] // mask_rows.shape[1]
    visible = jnp.repeat(jnp.repeat(mask_rows == 1, agent_block, axis=0), map_block, axis=1)
    probs, weights, attended = attend_forward(queries, keys, values, visible, scaling)
    attended_rounded = attended.astype(jnp.bfloat16)

    partial, w_far, attended_rounded = lax.optimization_barrier((partial, w_far, attended_rounded))
    with jax.named_scope("sum_over_y"):
        rows = tokens // (YH * YL)
        lines = lax.all_to_all(
            partial.reshape(YH * YL, rows, width), XY, 0, 0, axis_index_groups=y_groups()
        )
        summed = jnp.sum(lines.astype(jnp.float32), axis=0)
        row_keep = y * rows + jnp.arange(rows) < agent_count[0]
        own = jnp.where(row_keep[:, None], summed, 0.0).astype(jnp.bfloat16)
    with jax.named_scope("gather_attended"):
        attended_near = [attended_rounded] + [
            lax.ppermute(attended_rounded, "mp", shift_x(-k)) for k in range(1, X)
        ]

    own, attended_near = lax.optimization_barrier((own, attended_near))
    with jax.named_scope("gather_over_y"):
        spread = jnp.broadcast_to(own[None], (YH * YL, rows, width))
        block = lax.all_to_all(spread, XY, 0, 0, axis_index_groups=y_groups())
        block = block.reshape(tokens, width)
    with jax.named_scope("gather_projection"):
        w_near = jnp.stack(
            [w_far] + [lax.ppermute(w_far, "scene", shift_zl(-k)) for k in range(1, ZL)]
        )

    block, w_near = lax.optimization_barrier((block, w_near))
    with jax.named_scope("weight_terms"):
        send, keep = weight_terms(place, block, attended_near)

    with jax.named_scope("sum_over_core"):
        pair = sum_f32([keep, lax.ppermute(send, "scene", other_core())]).astype(jnp.bfloat16)

    with jax.named_scope("gather_projection"):
        w_other = lax.ppermute(w_near, "scene", other_core())

    pair, block = lax.optimization_barrier((pair, block))
    with jax.named_scope("gather_over_x"):
        spread = jnp.broadcast_to(block[None], (X, *block.shape))
        upstream = lax.all_to_all(spread, "mp", 0, 0, axis_index_groups=x_groups())

    with jax.named_scope("sum_over_z_lo"):
        parts = [
            lax.dynamic_index_in_dim(pair, (zl + k) & (ZL - 1), 0, keepdims=False)
            for k in range(ZL)
        ]
        near = sum_f32(
            parts[:1] + [lax.ppermute(parts[k], "scene", shift_zl(k)) for k in range(1, ZL)]
        ).astype(jnp.bfloat16)

    with jax.named_scope("sum_over_z_hi"):
        terms = [
            lax.ppermute(
                lax.dynamic_index_in_dim(near, (zh + k) & (X - 1), 0, keepdims=False),
                ("scene", "mp"),
                to_owner(k),
            )
            for k in range(ZH)
        ]

    with jax.named_scope("head_gradients"):
        upstream, w_other, _ = lax.optimization_barrier((upstream, w_other, near))
        d_attn = head_grad(place, upstream, w_near, w_other)
        d_queries, d_keys, d_values = attend_backward(
            queries, keys, values, d_attn, probs, weights, attended, scaling
        )
        terms, d_queries = lax.optimization_barrier((terms, d_queries))
        d_wout = sum_f32(terms)
    return d_queries[None], d_keys[None], d_values[None], d_wout


def solution(mesh):
    heads = P("scene", None, XY)
    return jax.shard_map(
        shards,
        mesh=mesh,
        in_specs=(
            P("scene", XY, None, None),
            heads,
            heads,
            heads,
            P(XY, "scene"),
            P("scene", None, None),
            P("scene"),
        ),
        out_specs=(heads, heads, heads, P(XY, "scene")),
        check_vma=False,
    )
```

```python
import math

import jax
import jax.numpy as jnp
from jax import lax
from jax.experimental import pallas as pl
from jax.experimental.pallas import tpu as pltpu
from jax.sharding import PartitionSpec as P

HEAD_DIM = 128
XY = ("section", "mp")
X, YH, YL = 4, 4, 2
ZH, ZL, CORES = 4, 4, 2


def xy_index(x, y):
    return (y % YL) * (X * YH) + x * YH + y // YL


def scene_index(zh, zl, core):
    return (zh * ZL + zl) * CORES + core


def shift_x(k):
    return [(x * YH + y, ((x + k) % X) * YH + y) for x in range(X) for y in range(YH)]


def shift_zl(k):
    return [
        (scene_index(a, b, c), scene_index(a, (b + k) % ZL, c))
        for a in range(ZH)
        for b in range(ZL)
        for c in range(CORES)
    ]


def z_lo_groups():
    return [
        [scene_index(a, b, c) for b in range(ZL)] for a in range(ZH) for c in range(CORES)
    ]


def z_hi_groups():
    return [
        [scene_index(a, b, c) for a in range(ZH)] for b in range(ZL) for c in range(CORES)
    ]


def swap_x_zh():
    pairs = []
    for a in range(ZH):
        for rest in range(ZL * CORES):
            for x in range(X):
                for yh in range(YH):
                    here = ((a * ZL * CORES + rest) * X + x) * YH + yh
                    there = ((x * ZL * CORES + rest) * X + a) * YH + yh
                    pairs.append((here, there))
    return pairs


def other_core():
    return [(s, s ^ 1) for s in range(ZH * ZL * CORES)]


def y_groups():
    return [[xy_index(x, y) for y in range(YH * YL)] for x in range(X)]


def attend_forward(queries, keys, values, visible, scaling):
    scores = jnp.einsum("qd,kd->qk", queries, keys, preferred_element_type=jnp.float32) * scaling
    scores = jnp.where(visible, scores, -1e30)
    largest = jnp.max(scores, axis=-1, keepdims=True)
    exponent = jnp.exp(scores - largest)
    probs = exponent / jnp.sum(exponent, axis=-1, keepdims=True)
    weights = probs.astype(jnp.bfloat16)
    attended = jnp.einsum("qk,kd->qd", weights, values, preferred_element_type=jnp.float32)
    return probs, weights, attended


def attend_backward(queries, keys, values, grads, probs, weights, attended, scaling):
    delta = jnp.sum(grads.astype(jnp.float32) * attended, axis=-1)
    d_values = jnp.einsum("qk,qd->kd", weights, grads, preferred_element_type=jnp.float32)
    d_probs = jnp.einsum("qd,kd->qk", grads, values, preferred_element_type=jnp.float32)
    score_grads = (probs * (d_probs - delta[:, None])).astype(jnp.bfloat16)
    d_queries = scaling * jnp.einsum(
        "qk,kd->qd", score_grads, keys, preferred_element_type=jnp.float32
    )
    d_keys = scaling * jnp.einsum(
        "qk,qd->kd", score_grads, queries, preferred_element_type=jnp.float32
    )
    return [g.astype(jnp.bfloat16) for g in (d_queries, d_keys, d_values)]


def add_own_kernel(x_ref, own_ref, *refs):
    *part_refs, out_ref = refs
    total = own_ref[...].astype(jnp.float32)
    for part_ref in part_refs:
        total += part_ref[...].astype(jnp.float32)
    out_ref[...] = total.astype(out_ref.dtype)


def add_own(x, sample, arrived):
    rows, width = arrived[0].shape
    whole = pl.BlockSpec((rows, width), lambda i, x: (0, 0))
    return pl.pallas_call(
        add_own_kernel,
        out_shape=jax.ShapeDtypeStruct((rows, width), jnp.bfloat16),
        grid_spec=pltpu.PrefetchScalarGridSpec(
            num_scalar_prefetch=1,
            grid=(1,),
            in_specs=[pl.BlockSpec((rows, width), lambda i, x: (0, x[0]))] + [whole] * (X - 1),
            out_specs=whole,
        ),
        compiler_params=pltpu.CompilerParams(vmem_limit_bytes=16 << 20),
        cost_estimate=pl.CostEstimate(
            flops=rows * width * X, bytes_accessed=2 * rows * width * (X + 1), transcendentals=0
        ),
        name="add_own",
    )(x.reshape(1), sample, *arrived)


def weight_terms_kernel(place_ref, block_ref, *refs):
    attended, (send_ref, keep_ref) = refs[:X], refs[X:]
    first = place_ref[0] == 0
    for k in range(X):
        head = (place_ref[1] + k) & (X - 1)
        term = lax.dot_general(
            attended[k][...],
            block_ref[...],
            (((0,), (0,)), ((), ())),
            preferred_element_type=jnp.float32,
        )
        for b in range(ZL):
            left = b * CORES * HEAD_DIM
            low = term[:, left : left + HEAD_DIM]
            high = term[:, left + HEAD_DIM : left + 2 * HEAD_DIM]
            send_ref[b, head] = jnp.where(first, high, low).astype(jnp.bfloat16)
            keep_ref[b, head] = jnp.where(first, low, high)


def weight_terms(place, block, attended):
    rows, width = block.shape
    shape = (ZL, X, HEAD_DIM, HEAD_DIM)
    vmem = pl.BlockSpec(memory_space=pltpu.VMEM)
    return pl.pallas_call(
        weight_terms_kernel,
        out_shape=(
            jax.ShapeDtypeStruct(shape, jnp.bfloat16),
            jax.ShapeDtypeStruct(shape, jnp.float32),
        ),
        in_specs=[pl.BlockSpec(memory_space=pltpu.SMEM)] + [vmem] * (1 + X),
        out_specs=(vmem, vmem),
        compiler_params=pltpu.CompilerParams(vmem_limit_bytes=24 << 20),
        cost_estimate=pl.CostEstimate(
            flops=2 * rows * width * X * HEAD_DIM,
            bytes_accessed=2 * rows * (width + X * HEAD_DIM) + 3 * width * X * HEAD_DIM,
            transcendentals=0,
        ),
        name="weight_terms",
    )(place, block, *attended)


def head_grad_kernel(place_ref, w_own_ref, w_other_ref, *refs):
    *blocks, out_ref = refs
    core, x, zl = [place_ref[i] for i in range(3)]
    total = jnp.zeros(out_ref.shape, jnp.float32)
    for k in range(X):
        far = (x + k) & (X - 1)
        for b in range(ZL):
            near = (b - zl) & (ZL - 1)
            left = b * CORES * HEAD_DIM
            own, other = w_own_ref[near, far], w_other_ref[near, far]
            first, second = jnp.where(core == 0, own, other), jnp.where(core == 0, other, own)
            for c, weight in enumerate((first, second)):
                total += lax.dot_general(
                    blocks[k][:, left + c * HEAD_DIM : left + (c + 1) * HEAD_DIM],
                    weight,
                    (((1,), (1,)), ((), ())),
                    preferred_element_type=jnp.float32,
                )
    out_ref[...] = total.astype(out_ref.dtype)


def head_grad(place, blocks, w_own, w_other):
    rows, width = blocks[0].shape
    vmem = pl.BlockSpec(memory_space=pltpu.VMEM)
    return pl.pallas_call(
        head_grad_kernel,
        out_shape=jax.ShapeDtypeStruct((rows, HEAD_DIM), jnp.bfloat16),
        in_specs=[pl.BlockSpec(memory_space=pltpu.SMEM)] + [vmem] * (2 + X),
        out_specs=vmem,
        compiler_params=pltpu.CompilerParams(vmem_limit_bytes=24 << 20),
        cost_estimate=pl.CostEstimate(
            flops=2 * rows * width * X * HEAD_DIM,
            bytes_accessed=2 * (rows + HEAD_DIM) * width * X,
            transcendentals=0,
        ),
        name="head_grad",
    )(place, w_own, w_other, *blocks)


def shift_right(number, size):
    return lax.shift_right_logical(number, size.bit_length() - 1)


def sum_f32(parts):
    total = parts[0].astype(jnp.float32)
    for k in range(1, len(parts)):
        total = total + parts[k].astype(jnp.float32)
    return total


def shards(dec_grad, agent_queries, map_keys, map_values, w_out, block_mask, agent_count):
    scaling = 1.0 / math.sqrt(HEAD_DIM)
    section, mp, scene = (lax.axis_index(name) for name in ("section", "mp", "scene"))
    x, y = shift_right(mp, YH), (mp & (YH - 1)) * YL + section
    zl = shift_right(scene, CORES) & (ZL - 1)
    core = scene & (CORES - 1)
    place = jnp.stack([core, x, zl])
    sample = dec_grad[0, 0]
    tokens, model = sample.shape
    width = model // X

    with jax.named_scope("sum_over_x"):
        pieces = [
            lax.dynamic_slice(sample, (0, ((x + k) & (X - 1)) * width), (tokens, width))
            for k in range(1, X)
        ]
        arrived = [lax.ppermute(piece, "mp", shift_x(k + 1)) for k, piece in enumerate(pieces)]
        partial = add_own(x, sample, arrived)

    with jax.named_scope("gather_projection"):
        w_spread = jnp.broadcast_to(w_out[None], (ZH, *w_out.shape))
        w_far = lax.all_to_all(w_spread, "scene", 0, 0, axis_index_groups=z_hi_groups())

    queries, keys, values = agent_queries[0], map_keys[0], map_values[0]
    mask_rows = block_mask[0]
    agent_block, map_block = tokens // mask_rows.shape[0], keys.shape[0] // mask_rows.shape[1]
    visible = jnp.repeat(jnp.repeat(mask_rows == 1, agent_block, axis=0), map_block, axis=1)
    probs, weights, attended = attend_forward(queries, keys, values, visible, scaling)
    attended_rounded = attended.astype(jnp.bfloat16)

    partial, w_far, attended_rounded = lax.optimization_barrier((partial, w_far, attended_rounded))
    with jax.named_scope("sum_over_y"):
        rows = tokens // (YH * YL)
        lines = lax.all_to_all(
            partial.reshape(YH * YL, rows, width), XY, 0, 0, axis_index_groups=y_groups()
        )
        summed = jnp.sum(lines.astype(jnp.float32), axis=0)
        row_keep = y * rows + jnp.arange(rows) < agent_count[0]
        own = jnp.where(row_keep[:, None], summed, 0.0).astype(jnp.bfloat16)
    with jax.named_scope("gather_attended"):
        attended_near = [attended_rounded] + [
            lax.ppermute(attended_rounded, "mp", shift_x(-k)) for k in range(1, X)
        ]

    own, attended_near = lax.optimization_barrier((own, attended_near))
    with jax.named_scope("gather_over_y"):
        spread = jnp.broadcast_to(own[None], (YH * YL, rows, width))
        block = lax.all_to_all(spread, XY, 0, 0, axis_index_groups=y_groups())
        block = block.reshape(tokens, width)
    with jax.named_scope("gather_projection"):
        w_near = jnp.stack(
            [w_far] + [lax.ppermute(w_far, "scene", shift_zl(-k)) for k in range(1, ZL)]
        )

    block, w_near = lax.optimization_barrier((block, w_near))
    with jax.named_scope("weight_terms"):
        send, keep = weight_terms(place, block, attended_near)

    with jax.named_scope("sum_over_core"):
        pair = sum_f32([keep, lax.ppermute(send, "scene", other_core())]).astype(jnp.bfloat16)

    with jax.named_scope("gather_projection"):
        w_other = lax.ppermute(w_near, "scene", other_core())

    with jax.named_scope("gather_over_x"):
        upstream = [block] + [lax.ppermute(block, "mp", shift_x(-k)) for k in range(1, X)]

    with jax.named_scope("sum_over_z_lo"):
        near = sum_f32(
            lax.all_to_all(pair, "scene", 0, 0, axis_index_groups=z_lo_groups())
        ).astype(jnp.bfloat16)

    with jax.named_scope("sum_over_z_hi"):
        summed_block = sum_f32(
            lax.all_to_all(near, "scene", 0, 0, axis_index_groups=z_hi_groups())
        )
        rounded = summed_block.astype(jnp.bfloat16)
        d_wout = lax.ppermute(rounded, ("scene", "mp"), swap_x_zh()).astype(jnp.float32)

    with jax.named_scope("head_gradients"):
        upstream, w_other, _ = lax.optimization_barrier((upstream, w_other, near))
        d_attn = head_grad(place, upstream, w_near, w_other)
        d_queries, d_keys, d_values = attend_backward(
            queries, keys, values, d_attn, probs, weights, attended, scaling
        )
    return d_queries[None], d_keys[None], d_values[None], d_wout


def solution(mesh):
    heads = P("scene", None, XY)
    return jax.shard_map(
        shards,
        mesh=mesh,
        in_specs=(
            P("scene", XY, None, None),
            heads,
            heads,
            heads,
            P(XY, "scene"),
            P("scene", None, None),
            P("scene"),
        ),
        out_specs=(heads, heads, heads, P(XY, "scene")),
        check_vma=False,
    )
```
